256 devices in a mesh: lat: 16 (over y, x), lon: 16 (over z, core).
Axes of the slice: x: 4, y: 4, z: 8, core: 2. Of those that a mesh axis runs over, the one named last changes fastest.
Arguments:
- innovation: float32 [64, 16384], P(None, ('lat', 'lon')), may hold values from -6 to 6
- obs_weight: float32 [64, 16384], P(None, ('lat', 'lon')), may hold values from 0.5 to 4
- jacobian: float32 [49152, 64, 128], P(('lat', 'lon')), may hold values from -0.5 to 0.5
- block_list: int32 [2, 49152], P(None, ('lat', 'lon')), may hold values from 0 to 1024, as said below
- pass_counts: int32 [2], replicated, may hold values from 3 to 6, as said below
- kappa_h: float32 [256, 512, 128], P('lat', 'lon'), may hold values from 0.03 to 0.24
- kappa_v: float32 [256, 512, 128], P('lat', 'lon'), may hold values from 0.05 to 0.45
Outputs:
- increment: float32 [256, 512, 128], P('lat', 'lon')
- residual: float32 [256, 512, 128], P('lat', 'lon')
The draws below stay inside these ranges and needn't reach their ends.
Inputs may be any that keep to these rules, and one draw needn't show every extreme that they name: `pass_counts`: entry 0 counts lateral passes and entry 1 vertical passes; one of the two is 6 and the other is smaller. `block_list`: on each device the non-empty slots come first among its 192 slots, and in every latitude band some device has all 192 slots non-empty; an empty slot has block row 1024.
All inputs are finite; a program needn't handle non-finite values.
Results may differ from the reference program's by a relative error of at most 0.0003.
Values sent between devices are 32-bit elements; how exact they have to be, the bound alone decides.
A program may use at most 64 MiB of HBM per device.

```python
import math
import jax
import jax.numpy as jnp
from jax import lax

CLAT = 16
CLON = 32
LEVELS = 128
OBSB = 64
ROWS_DEV = 64
CAP = 192
PASS_MIN = 3
PASS_MAX = 6
ITERS = 2
NLAT = 256
NLON = 512
ROWS_LAT = 1024
OBSROWS = 16384
BLOCKS = 49152
N_LAT = 16
N_LON = 16


def draw_block_list(key, part):
    subkeys = jax.random.split(jax.random.fold_in(key, 41), 4)
    device_count = BLOCKS // CAP
    lon_count = ROWS_LAT // ROWS_DEV
    band_count = device_count // lon_count
    loaded = jax.random.randint(subkeys[0], (device_count,), CAP // 8, CAP // 2 + 1)
    busiest = jax.random.randint(subkeys[1], (band_count, 1), 0, lon_count)
    position = jnp.arange(lon_count, dtype=jnp.int32)[None, :]
    crowded = ((position == busiest) | (position == (busiest + 1) % lon_count)).reshape(-1)
    loaded = jnp.where(crowded, CAP, loaded)
    slot_ids = jnp.arange(CAP, dtype=jnp.int32)[None, :]
    active = slot_ids < loaded[:, None]
    row_ids = jax.random.randint(subkeys[2], (device_count, CAP), 0, ROWS_LAT)
    row_ids = jnp.where(active, row_ids, ROWS_LAT)
    col_ids = jax.random.randint(subkeys[3], (device_count, CAP), 0, CLAT * CLON)
    return jnp.stack([row_ids.reshape(-1), col_ids.reshape(-1)]).astype(jnp.int32)


def draw_pass_counts(key, part):
    subkeys = jax.random.split(jax.random.fold_in(key, 23), 2)
    drawn = jax.random.randint(subkeys[0], (2,), PASS_MIN, PASS_MAX)
    chosen = jax.random.randint(subkeys[1], (), 0, 2)
    return jnp.where(jnp.arange(2) == chosen, PASS_MAX, drawn).astype(jnp.int32)


def block_scale(rng, dims, cuts, smallest, high):
    factor_of, own = 1.0, jax.random.fold_in(rng, 6)
    for axis_at, blocks in cuts:
        heights = jnp.exp(jax.random.uniform(jax.random.fold_in(own, axis_at), (blocks,), jnp.float32, smallest / len(cuts), high / len(cuts)))
        factor_of = factor_of * jnp.repeat(heights, dims[axis_at] // blocks).reshape([-1 if axis == axis_at else 1 for axis in range(len(dims))])
    return factor_of


def scatter_about(key, extent, scale, most, cuts=(), kind=jnp.bfloat16):
    entries = scale * jax.random.normal(key, extent, jnp.float32)
    if cuts:
        entries = entries * block_scale(key, extent, cuts, -0.22, 0.18)
    return jnp.clip(entries, -most, most).astype(kind)


def setup_inputs(seed: int = 0) -> dict:
    key_of = jax.random.split(jax.random.key(seed), 8)
    innovation = scatter_about(key_of[0], (OBSB, OBSROWS), 1.0, 6.0, ((1, 256),), jnp.float32)
    obs_weight = jnp.clip(jnp.exp(math.log(4.0) - 2.0794415 * jax.random.uniform(key_of[1], (OBSB, OBSROWS), jnp.float32) ** block_scale(key_of[1], (OBSB, OBSROWS), ((1, 256),), -0.2, 0.2)), 0.5, 4.0)
    jacobian = scatter_about(key_of[2], (BLOCKS, OBSB, LEVELS), LEVELS ** -0.5, 0.5, ((0, 256),), jnp.float32)
    block_list = draw_block_list(jax.random.fold_in(key_of[7], 71), 0)
    pass_counts = draw_pass_counts(jax.random.fold_in(key_of[7], 71), 0)
    kappa_h = jnp.clip(jnp.exp(math.log(0.24) - 2.0794415 * jax.random.uniform(key_of[5], (NLAT, NLON, LEVELS), jnp.float32) ** block_scale(key_of[5], (NLAT, NLON, LEVELS), ((0, 16), (1, 16)), -0.2, 0.2)), 0.03, 0.24)
    kappa_v = jnp.clip(jnp.exp(math.log(0.45) - 2.1972245 * jax.random.uniform(key_of[6], (NLAT, NLON, LEVELS), jnp.float32) ** block_scale(key_of[6], (NLAT, NLON, LEVELS), ((0, 16), (1, 16)), -0.2, 0.2)), 0.05, 0.45)
    return {"innovation": innovation, "obs_weight": obs_weight, "jacobian": jacobian, "block_list": block_list, "pass_counts": pass_counts, "kappa_h": kappa_h, "kappa_v": kappa_v}


def vertical_faces(kappa_v):
    upper_face = jnp.sqrt(kappa_v[..., :-1] * kappa_v[..., 1:])
    zero_face = jnp.zeros(kappa_v.shape[:-1] + (1,), jnp.float32)
    return (jnp.concatenate([upper_face, zero_face], -1), jnp.concatenate([zero_face, upper_face], -1))

def vertical_pass(current, face_below, face_above):
    zero_face = jnp.zeros(current.shape[:-1] + (1,), jnp.float32)
    higher = jnp.concatenate([current[..., 1:], zero_face], -1)
    lower_level = jnp.concatenate([zero_face, current[..., :-1]], -1)
    return current + face_below * (higher - current) + face_above * (lower_level - current)

def lateral_faces(kappa_h):
    padded = jnp.pad(kappa_h, ((1, 1), (0, 0), (0, 0)))
    return (jnp.sqrt(kappa_h * padded[:-2]), jnp.sqrt(kappa_h * padded[2:]), jnp.sqrt(kappa_h * jnp.roll(kappa_h, 1, axis=1)), jnp.sqrt(kappa_h * jnp.roll(kappa_h, -1, axis=1)))

def lateral_pass(current, face_set):
    padded = jnp.pad(current, ((1, 1), (0, 0), (0, 0)))
    return current + face_set[0] * (padded[:-2] - current) + face_set[1] * (padded[2:] - current) + face_set[2] * (jnp.roll(current, 1, axis=1) - current) + face_set[3] * (jnp.roll(current, -1, axis=1) - current)

def reference(innovation, obs_weight, jacobian, block_list, pass_counts, kappa_h, kappa_v):
    lateral_count = pass_counts[0]
    vertical_count = pass_counts[1]
    face_set = lateral_faces(kappa_h)
    face_below, face_above = vertical_faces(kappa_v)

    def vertical(current):
        return lax.fori_loop(0, vertical_count, lambda counter, running: vertical_pass(running, face_below, face_above), current)

    def lateral(current):
        return lax.fori_loop(0, lateral_count, lambda counter, running: lateral_pass(running, face_set), current)

    def spread(current):
        return lateral(vertical(current))

    def spread_adjoint(current):
        return vertical(lateral(current))
    device_count = N_LAT * N_LON
    column_count = CLAT * CLON

    def to_columns(current):
        return current.reshape(N_LAT, CLAT, N_LON, CLON, LEVELS).transpose(0, 2, 1, 3, 4).reshape(device_count * column_count, LEVELS)

    def from_columns(columns):
        return columns.reshape(N_LAT, N_LON, CLAT, CLON, LEVELS).transpose(0, 2, 1, 3, 4).reshape(NLAT, NLON, LEVELS)
    block_rows = block_list[0].reshape(device_count, CAP)
    block_cols = block_list[1].reshape(device_count, CAP)
    active = block_rows < ROWS_LAT
    band_index = (jnp.arange(device_count, dtype=jnp.int32) // N_LON)[:, None]
    obs_ids = jnp.where(active, band_index * ROWS_LAT + block_rows, 0).astype(jnp.int32).reshape(-1)
    cell_ids = (jnp.arange(device_count, dtype=jnp.int32)[:, None] * column_count + block_cols).astype(jnp.int32).reshape(-1)
    active_mask = active.reshape(-1).astype(jnp.float32)[:, None]

    def observe(current):
        picked = to_columns(current)[cell_ids]
        block_obs = jnp.einsum('bok,bk->bo', jacobian, picked, precision=lax.Precision.HIGHEST) * active_mask
        return jax.ops.segment_sum(block_obs, obs_ids, num_segments=OBSROWS).T

    def observe_adjoint(weighted):
        taken = weighted.T[obs_ids] * active_mask
        contrib = jnp.einsum('bok,bo->bk', jacobian, taken, precision=lax.Precision.HIGHEST)
        return from_columns(jax.ops.segment_sum(contrib, cell_ids, num_segments=device_count * column_count))
    gradient = spread_adjoint(observe_adjoint(obs_weight * innovation))
    solution = jnp.zeros_like(gradient)
    residual = gradient
    direction = gradient
    norm_now = jnp.sum(residual * residual)
    for iteration in range(ITERS):
        image_vec = direction + spread_adjoint(observe_adjoint(obs_weight * observe(spread(direction))))
        alpha_step = norm_now / jnp.sum(direction * image_vec)
        solution = solution + alpha_step * direction
        residual = residual - alpha_step * image_vec
        if iteration + 1 < ITERS:
            norm_next = jnp.sum(residual * residual)
            direction = residual + norm_next / norm_now * direction
            norm_now = norm_next
    return (spread(solution), residual)
```

```python
import functools

import jax
import jax.numpy as jnp
from jax import lax
from jax.experimental import pallas as pl
from jax.experimental.pallas import tpu as pltpu
from jax.sharding import PartitionSpec as P

MOST = 6
LEAST = 3
SIDE = 8
F32 = jnp.float32
BF16 = jnp.bfloat16
MOVES = tuple((i, j) for i in (-1, 0, 1) for j in (-1, 0, 1) if (i, j) != (0, 0))


def split(value):
    high = value.astype(BF16)
    return high, (value - high.astype(F32)).astype(BF16)


def dot2(left, right):
    high, low = split(left)
    return jnp.dot(high, right, preferred_element_type=F32) + jnp.dot(
        low, right, preferred_element_type=F32
    )


def dot2r(left, right):
    high, low = split(right)
    return jnp.dot(left, high, preferred_element_type=F32) + jnp.dot(
        left, low, preferred_element_type=F32
    )


def kernel(
    shape, counts, cols, rows_in, innov, weight, jac_in, kh_in, kv,
    increment, residual_out,
    jac, kap, ext, tmp, lco, vco, lst, rhot, rhott, chot, contrib,
    grad, resid, evolved, pair_out, pair_in, wide,
    zbuf, zsib, zchip, zin, zown, band, lat_out, lat_in,
    local_sem, halo_s, halo_r, pair_s, pair_r, sib_s, sib_r, rs_s, rs_r,
    ag_s, ag_r, fw_s, fw_r, lat_s, lat_r,
):
    n_lat, n_lon, cells_i, cells_j, levels, slots, obs = shape
    chips = n_lon // 2
    half = obs // 2
    span = cells_j + 2 * SIDE
    total_rows = cells_i + 2 * MOST
    a = lax.axis_index("lat")
    b = lax.axis_index("lon")
    chip = b // 2
    core = lax.rem(b, 2)
    sibling = chip * 2 + 1 - core
    lat_of = lambda d: lax.rem(a + d + n_lat, n_lat)
    lon_of = lambda d: lax.rem(b + d + n_lon, n_lon)
    chip_of = lambda d: lax.rem(chip + d + chips, chips)
    started = []

    def remote(src, dst, ss, rs, to_lat, to_lon):
        copy = pltpu.make_async_remote_copy(
            src_ref=src, dst_ref=dst, send_sem=ss, recv_sem=rs,
            device_id=(to_lat, to_lon), device_id_type=pl.DeviceIdType.MESH,
        )
        copy.start()
        started.append(copy)
        return copy

    rows_src = {-1: slice(MOST, 2 * MOST), 0: slice(MOST, MOST + cells_i), 1: slice(cells_i, cells_i + MOST)}
    rows_dst = {-1: slice(MOST + cells_i, total_rows), 0: slice(MOST, MOST + cells_i), 1: slice(0, MOST)}
    cols_src = {-1: slice(SIDE, 2 * SIDE), 0: slice(SIDE, SIDE + cells_j), 1: slice(cells_j, cells_j + SIDE)}
    cols_dst = {-1: slice(SIDE + cells_j, span), 0: slice(SIDE, SIDE + cells_j), 1: slice(0, SIDE)}

    def halo(ref, which):
        return [
            remote(
                ref.at[rows_src[i], cols_src[j], :], ref.at[rows_dst[i], cols_dst[j], :],
                halo_s.at[which, m], halo_r.at[which, m], lat_of(i), lon_of(j),
            )
            for m, (i, j) in enumerate(MOVES)
        ]

    jac_copy = pltpu.make_async_copy(jac_in, jac, local_sem.at[0])
    jac_copy.start()
    kap_copy = pltpu.make_async_copy(
        kh_in, kap.at[MOST:MOST + cells_i, SIDE:SIDE + cells_j, :], local_sem.at[1]
    )
    kap_copy.start()

    partners = [(lat_of(i), lon_of(j)) for i, j in MOVES]
    partners += [(lat_of(d), b) for d in range(2, n_lat - 1)]
    partners += [(a, chip_of(d) * 2 + core) for d in range(1, chips)]
    partners += [(a, sibling)]
    barrier = pltpu.get_barrier_semaphore()
    for to_lat, to_lon in partners:
        pl.semaphore_signal(
            barrier, inc=1, device_id=(to_lat, to_lon), device_id_type=pl.DeviceIdType.MESH
        )

    pair_out[0] = weight[...] * innov[...]
    pair_out[1] = weight[...]

    lst[...] = jnp.full(lst.shape, n_lon * obs, jnp.int32)
    lst[0:2, 0:slots] = rows_in[...]
    padded = lst.shape[1]
    row_line = lst[0:1, :]
    col_line = lst[1:2, :]
    lane = lax.broadcasted_iota(jnp.int32, (padded, 128), 1)
    row_column = jnp.transpose(jnp.broadcast_to(row_line.astype(F32), (128, padded))).astype(jnp.int32)
    for c in range(chips):
        rhot[:, 128 * c:128 * c + 128] = jnp.where(row_column == lane + 128 * c, 1.0, 0.0).astype(BF16)
    sub = lax.broadcasted_iota(jnp.int32, (128, padded), 0)
    for c in range(chips):
        rhott[128 * c:128 * c + 128, :] = jnp.where(row_line == sub + 128 * c, 1.0, 0.0).astype(BF16)
    for c in range(cells_i * cells_j // 128):
        chot[128 * c:128 * c + 128, :] = jnp.where(
            (col_line == sub + 128 * c) & (row_line < n_lon * obs), 1.0, 0.0
        ).astype(BF16)
    contrib[slots:padded, :] = jnp.zeros((padded - slots, levels), F32)

    pl.semaphore_wait(barrier, len(partners))
    pair = remote(pair_out, pair_in, pair_s, pair_r, a, sibling)
    kap_copy.wait()
    kap_moves = halo(kap, 0)

    level = lax.broadcasted_iota(jnp.int32, (cells_j, levels), 1)

    @pl.loop(0, cells_i)
    def _(i):
        root = jnp.sqrt(kv[i])
        below = jnp.where(level < levels - 1, root * pltpu.roll(root, levels - 1, 1), 0.0)
        above = jnp.where(level > 0, root * pltpu.roll(root, 1, 1), 0.0)
        vco[0, i] = 1.0 - below - above
        vco[1, i] = below
        vco[2, i] = above

    lateral_count = jnp.full((span, levels), counts[0], jnp.int32)
    vertical_count = jnp.full((cells_j, levels), counts[1], jnp.int32)

    def vertical(i, w):
        keep, below, above = vco[0, i], vco[1, i], vco[2, i]
        for p in range(MOST):
            new = keep * w + below * pltpu.roll(w, levels - 1, 1) + above * pltpu.roll(w, 1, 1)
            w = new if p < LEAST else jnp.where(vertical_count > p, new, w)
        return w

    def lateral(field, post):
        source = ext.at[field]
        for p in range(MOST):
            last = p == MOST - 1
            target = tmp.at[p % 2]
            begin = p + 1

            @pl.loop(0, (total_rows - 2 * begin) // 2)
            def _(g, source=source, target=target, p=p, last=last, begin=begin):
                for u in range(2):
                    i = begin + 2 * g + u
                    w = source[i]
                    new = (
                        lco[0, i] * w + lco[1, i] * source[i - 1] + lco[2, i] * source[i + 1]
                        + lco[3, i] * pltpu.roll(w, 1, 0) + lco[4, i] * pltpu.roll(w, span - 1, 0)
                    )
                    if p >= LEAST:
                        new = jnp.where(lateral_count > p, new, w)
                    if last:
                        post(i - MOST, new[SIDE:SIDE + cells_j, :])
                    else:
                        target[i] = new
            source = target

    def put_band(r, piece, tile):
        band[r, core, chip, 0:half, :] = piece
        band[r, core, chip, half:half + 8, :] = tile
        mine = band.at[r, core, chip]
        order = sorted(range(1, chips), key=lambda d: -min(d, chips - d))
        sent = {
            d: remote(mine, mine, ag_s.at[r, d], ag_r.at[r, d], a, chip_of(d) * 2 + core)
            for d in order
        }
        forwards = [remote(mine, mine, fw_s.at[r, 0], fw_r.at[r, 0], a, sibling)]
        for d in reversed(order):
            sent[d].wait_recv()
            arrived = band.at[r, core, chip_of(-d)]
            forwards.append(remote(arrived, arrived, fw_s.at[r, d], fw_r.at[r, d], a, sibling))
        for copy in forwards:
            copy.wait_recv()

    def band_matrix(r):
        return jnp.concatenate(
            [
                jnp.concatenate([band[r, h, c, 0:half, :] for c in range(chips)], axis=1)
                for h in range(2)
            ],
            axis=0,
        )

    def band_tile(r):
        tile = band[r, 0, 0, half:half + 8, :]
        for h in range(2):
            for c in range(chips):
                if h or c:
                    tile = tile + band[r, h, c, half:half + 8, :]
        return tile

    def send_lat(i, tile):
        lat_out[i] = tile
        return [
            remote(lat_out.at[i], lat_in.at[i, d - 1], lat_s.at[i, d - 1], lat_r.at[i, d - 1], lat_of(d), b)
            for d in range(1, n_lat)
        ]

    def sum_lat(i, copies):
        tile = lat_out[i]
        for d, copy in enumerate(copies):
            copy.wait_recv()
            tile = tile + lat_in[i, d]
        return tile

    def adjoint(r, field):
        taken = dot2(band_matrix(r), rhott[...])
        for block in range(0, slots, 128):
            count = min(128, slots - block)
            part = taken[:, block:block + 128]

            def body(g, part, block=block):
                first = pl.multiple_of(block + 8 * g, 8)
                lines = []
                for u in range(8):
                    product = jac[first + u] * jnp.broadcast_to(part[:, u:u + 1], (obs, levels))
                    lines.append(jnp.sum(product, axis=0, keepdims=True))
                contrib[pl.ds(first, 8), :] = jnp.concatenate(lines, axis=0)
                return pltpu.roll(part, 120, 1)

            lax.fori_loop(0, count // 8, body, part)
        columns = dot2r(chot[...], contrib[...])
        for i in range(cells_i):
            ext[field, MOST + i, SIDE:SIDE + cells_j, :] = columns[cells_j * i:cells_j * i + cells_j, :]

    def observe(which, r, tile):
        lane_of = lax.broadcasted_iota(jnp.int32, (obs, 128), 1)
        parts = []
        for block in range(0, slots, 128):
            count = min(128, slots - block)

            def body(g, acc, block=block):
                for u in range(8):
                    s = block + 8 * g + u
                    column = jnp.minimum(cols[1, s], cells_i * cells_j - 1)
                    line = evolved[which, pl.ds(column, 1), :]
                    value = jnp.sum(jac[s] * line, axis=1, keepdims=True)
                    acc = jnp.where(lane_of == 8 * g + u, value, acc)
                return acc

            parts.append(lax.fori_loop(0, count // 8, body, jnp.zeros((obs, 128), F32)))
        partial = dot2(jnp.concatenate(parts, axis=1), rhot[...])
        for h in range(2):
            for c in range(chips):
                zbuf[r, h, c, 0:half, :] = partial[half * h:half * h + half, 128 * c:128 * c + 128]
                zbuf[r, h, c, half:half + 8, :] = tile
        remote(zbuf.at[r, 1 - core], zsib.at[r], sib_s.at[r], sib_r.at[r], a, sibling).wait_recv()
        for c in range(chips):
            zchip[r, c] = zbuf[r, core, c] + zsib[r, c]
        order = sorted(range(1, chips), key=lambda d: -min(d, chips - d))
        copies = [
            remote(
                zchip.at[r, chip_of(d)], zin.at[r, d - 1], rs_s.at[r, d - 1], rs_r.at[r, d - 1],
                a, chip_of(d) * 2 + core,
            )
            for d in order
        ]
        total = zchip[r, chip]
        for copy in copies:
            copy.wait_recv()
        for d in range(1, chips):
            total = total + zin[r, d - 1]
        return total[0:half, :], total[half:half + 8, :]

    def fold(value):
        return jnp.sum(value.reshape(value.shape[0] // 8, 8, levels), axis=0)

    def whole(value):
        return jnp.sum(jnp.sum(value, axis=0, keepdims=True), axis=1, keepdims=True)

    pair.wait_recv()
    for q in range(2):
        own, other = pair_out[q], pair_in[q]
        wide[q] = jnp.concatenate(
            [jnp.where(core == 0, own, other), jnp.where(core == 0, other, own)], axis=1
        )
    offset = pl.multiple_of(core * half, half)
    put_band(0, wide[0, pl.ds(offset, half), :], jnp.zeros((8, levels), F32))
    weight_own = wide[1, pl.ds(offset, half), :]
    jac_copy.wait()
    adjoint(0, 0)
    moves = halo(ext.at[0], 1)

    for copy in kap_moves:
        copy.wait_recv()
    north = jnp.where(a == 0, 0.0, 1.0)
    south = jnp.where(a == n_lat - 1, 0.0, 1.0)
    for i in range(MOST):
        kap[i] = kap[i] * north
        kap[MOST + cells_i + i] = kap[MOST + cells_i + i] * south

    @pl.loop(0, total_rows)
    def _(i):
        tmp[0, i] = jnp.sqrt(kap[i])

    @pl.loop(1, total_rows - 1)
    def _(i):
        root = tmp[0, i]
        up = root * tmp[0, i - 1]
        down = root * tmp[0, i + 1]
        west = root * pltpu.roll(root, 1, 0)
        east = root * pltpu.roll(root, span - 1, 0)
        lco[0, i] = 1.0 - (up + down + west + east)
        lco[1, i] = up
        lco[2, i] = down
        lco[3, i] = west
        lco[4, i] = east

    def wait_halo(copies):
        for copy in copies:
            copy.wait_recv()

    def middle(field, i):
        return ext.at[field, MOST + i, SIDE:SIDE + cells_j, :]

    zero_tile = jnp.zeros((8, levels), F32)
    acc_a = lat_out.at[4]
    acc_b = lat_out.at[5]
    wait_halo(moves)
    acc_a[...] = zero_tile

    def post_gradient(i, w):
        w = vertical(i, w)
        grad[i] = w
        acc_a[...] += fold(w * w)
        ext[1, MOST + i, SIDE:SIDE + cells_j, :] = vertical(i, w)

    lateral(0, post_gradient)
    norm_copies = send_lat(0, acc_a[...])
    wait_halo(halo(ext.at[1], 2))

    def post_evolved(which, i, w):
        evolved[which, pl.ds(pl.multiple_of(i * cells_j, cells_j), cells_j), :] = w

    lateral(1, functools.partial(post_evolved, 0))

    piece, tile = observe(0, 0, sum_lat(0, norm_copies))
    norm = whole(tile)
    zown[...] = piece
    weighted = weight_own * piece
    put_band(1, weighted, fold(weighted * piece))
    curve_copies = send_lat(1, band_tile(1))
    adjoint(1, 2)
    moves = halo(ext.at[2], 3)
    alpha_first = norm / (norm + whole(sum_lat(1, curve_copies)))
    alpha_wide = jnp.broadcast_to(alpha_first, (cells_j, levels))
    wait_halo(moves)
    acc_a[...] = zero_tile
    acc_b[...] = zero_tile

    def post_residual(i, w):
        g = grad[i]
        new = g - alpha_wide * (g + vertical(i, w))
        resid[i] = new
        acc_a[...] += fold(new * new)
        acc_b[...] += fold(new * g)
        ext[3, MOST + i, SIDE:SIDE + cells_j, :] = vertical(i, new)

    lateral(2, post_residual)
    sub8 = lax.broadcasted_iota(jnp.int32, (8, levels), 0)
    norm_copies = send_lat(
        2,
        jnp.where(
            sub8 == 0,
            jnp.sum(acc_a[...], axis=0, keepdims=True),
            jnp.where(sub8 == 1, jnp.sum(acc_b[...], axis=0, keepdims=True), 0.0),
        ),
    )
    wait_halo(halo(ext.at[3], 4))
    lateral(3, functools.partial(post_evolved, 1))

    piece, tile = observe(1, 1, sum_lat(2, norm_copies))
    norm_next = jnp.sum(tile[0:1, :], axis=1, keepdims=True)
    cross = jnp.sum(tile[1:2, :], axis=1, keepdims=True)
    beta = norm_next / norm
    square = norm_next + 2.0 * beta * cross + beta * beta * norm
    piece = piece + beta * zown[...]
    weighted = weight_own * piece
    put_band(2, weighted, fold(weighted * piece))
    curve_copies = send_lat(3, band_tile(2))
    adjoint(2, 4)
    moves = halo(ext.at[4], 5)
    alpha_second = norm_next / (square + whole(sum_lat(3, curve_copies)))
    second_wide = jnp.broadcast_to(alpha_second, (cells_j, levels))
    beta_wide = jnp.broadcast_to(beta, (cells_j, levels))
    wait_halo(moves)

    def post_last(i, w):
        r = resid[i]
        residual_out[i] = r - second_wide * (r + beta_wide * grad[i] + vertical(i, w))
        place = pl.ds(pl.multiple_of(i * cells_j, cells_j), cells_j)
        first, second = evolved[0, place, :], evolved[1, place, :]
        increment[i] = alpha_wide * first + second_wide * (second + beta_wide * first)

    lateral(4, post_last)
    for copy in started:
        copy.wait_send()


def local(n_lat, n_lon, innovation, obs_weight, jacobian, block_list, pass_counts, kappa_h, kappa_v):
    cells_i, cells_j, levels = kappa_h.shape
    slots, obs, _ = jacobian.shape
    shape = (n_lat, n_lon, cells_i, cells_j, levels, slots, obs)
    chips = n_lon // 2
    half = obs // 2
    span = cells_j + 2 * SIDE
    total_rows = cells_i + 2 * MOST
    padded = -(-slots // 128) * 128
    columns = cells_i * cells_j
    vmem = pltpu.VMEM
    dma = pltpu.SemaphoreType.DMA
    field = jax.ShapeDtypeStruct((cells_i, cells_j, levels), F32)
    in_vmem = pl.BlockSpec(memory_space=pltpu.VMEM)
    in_smem = pl.BlockSpec(memory_space=pltpu.SMEM)
    in_any = pl.BlockSpec(memory_space=pl.ANY)
    return pl.pallas_call(
        functools.partial(kernel, shape),
        out_shape=(field, field),
        in_specs=[in_smem, in_smem, in_vmem, in_vmem, in_vmem, in_any, in_any, in_vmem],
        out_specs=(in_vmem, in_vmem),
        scratch_shapes=[
            vmem((slots, obs, levels), F32),
            vmem((total_rows, span, levels), F32),
            vmem((5, total_rows, span, levels), F32),
            vmem((2, total_rows, span, levels), F32),
            vmem((5, total_rows, span, levels), F32),
            vmem((3, cells_i, cells_j, levels), F32),
            vmem((8, padded), jnp.int32),
            vmem((padded, 128 * chips), BF16),
            vmem((128 * chips, padded), BF16),
            vmem((columns, padded), BF16),
            vmem((padded, levels), F32),
            vmem((cells_i, cells_j, levels), F32),
            vmem((cells_i, cells_j, levels), F32),
            vmem((2, columns, levels), F32),
            vmem((2, obs, obs), F32),
            vmem((2, obs, obs), F32),
            vmem((2, obs, 2 * obs), F32),
            vmem((2, 2, chips, half + 8, 128), F32),
            vmem((2, chips, half + 8, 128), F32),
            vmem((2, chips, half + 8, 128), F32),
            vmem((2, chips - 1, half + 8, 128), F32),
            vmem((half, 128), F32),
            vmem((3, 2, chips, half + 8, 128), F32),
            vmem((6, 8, 128), F32),
            vmem((4, n_lat - 1, 8, 128), F32),
            dma((2,)),
            dma((6, 8)), dma((6, 8)),
            dma, dma,
            dma((2,)), dma((2,)),
            dma((2, chips - 1)), dma((2, chips - 1)),
            dma((3, chips)), dma((3, chips)),
            dma((3, chips)), dma((3, chips)),
            dma((4, n_lat - 1)), dma((4, n_lat - 1)),
        ],
        compiler_params=pltpu.CompilerParams(
            collective_id=0, has_side_effects=True, vmem_limit_bytes=60 * 1024 * 1024
        ),
    )(pass_counts, block_list, block_list, innovation, obs_weight, jacobian, kappa_h, kappa_v)


def solution(mesh):
    return jax.shard_map(
        functools.partial(local, mesh.shape["lat"], mesh.shape["lon"]),
        mesh=mesh,
        in_specs=(
            P(None, ("lat", "lon")),
            P(None, ("lat", "lon")),
            P(("lat", "lon"), None, None),
            P(None, ("lat", "lon")),
            P(),
            P("lat", "lon", None),
            P("lat", "lon", None),
        ),
        out_specs=(P("lat", "lon", None), P("lat", "lon", None)),
        check_vma=False,
    )
```

```python
import functools

import jax
import jax.numpy as jnp
from jax import lax
from jax.experimental import pallas as pl
from jax.experimental.pallas import tpu as pltpu
from jax.sharding import PartitionSpec as P

MOST = 6
LEAST = 3
SIDE = 8
F32 = jnp.float32
BF16 = jnp.bfloat16
MOVES = tuple((i, j) for i in (-1, 0, 1) for j in (-1, 0, 1) if (i, j) != (0, 0))


def split(value):
    high = value.astype(BF16)
    return high, (value - high.astype(F32)).astype(BF16)


def pick(table, value):
    both = jnp.concatenate(split(value), axis=1)
    out = jnp.dot(table, both, preferred_element_type=F32)
    width = value.shape[1]
    return out[:, :width], out[:, width:]


def kernel(
    shape, counts, rows_in, innov, weight, jac_in, kh_in, kv,
    increment, residual_out,
    jac, jparts, jturn, kap, ext, tmp, lco, vco, lst, rsel, rselt, chot, chott, lhs, contrib, observed,
    done, grad, resid, evolved, square,
    zbuf, zsib, zchip, zin, zown, wown, band, sum_out, sum_in,
    local_sem, halo_s, halo_r, sib_s, sib_r, rs_s, rs_r,
    ag_s, ag_r, fw_s, fw_r, sum_s, sum_r,
):
    n_lat, n_lon, cells_i, cells_j, levels, slots, obs = shape
    chips = n_lon // 2
    half = obs // 2
    span = cells_j + 2 * SIDE
    total_rows = cells_i + 2 * MOST
    columns = cells_i * cells_j
    a = lax.axis_index("lat")
    b = lax.axis_index("lon")
    chip = b // 2
    core = lax.rem(b, 2)
    sibling = chip * 2 + 1 - core
    lat_of = lambda d: lax.rem(a + d + n_lat, n_lat)
    lon_of = lambda d: lax.rem(b + d + n_lon, n_lon)
    chip_of = lambda d: lax.rem(chip + d + chips, chips)
    started = []

    def describe(src, dst, ss, rs, to_lat, to_lon):
        return pltpu.make_async_remote_copy(
            src_ref=src, dst_ref=dst, send_sem=ss, recv_sem=rs,
            device_id=(to_lat, to_lon), device_id_type=pl.DeviceIdType.MESH,
        )

    def remote(*args):
        copy = describe(*args)
        copy.start()
        started.append(copy)
        return copy

    rows_src = {-1: slice(MOST, 2 * MOST), 0: slice(MOST, MOST + cells_i), 1: slice(cells_i, cells_i + MOST)}
    rows_dst = {-1: slice(MOST + cells_i, total_rows), 0: slice(MOST, MOST + cells_i), 1: slice(0, MOST)}
    cols_src = {-1: slice(SIDE, 2 * SIDE), 0: slice(SIDE, SIDE + cells_j), 1: slice(cells_j, cells_j + SIDE)}
    cols_dst = {-1: slice(SIDE + cells_j, span), 0: slice(SIDE, SIDE + cells_j), 1: slice(0, SIDE)}
    sends = {-1: a > 0, 1: a < n_lat - 1}
    gets = {-1: a < n_lat - 1, 1: a > 0}

    def halo_copy(ref, which, m):
        i, j = MOVES[m]
        return describe(
            ref.at[rows_src[i], cols_src[j], :], ref.at[rows_dst[i], cols_dst[j], :],
            halo_s.at[which, m], halo_r.at[which, m], lat_of(i), lon_of(j),
        )

    def halo_send(ref, which, toward):
        picked = [m for m in range(len(MOVES)) if MOVES[m][0] == toward]

        def start():
            for m in picked:
                halo_copy(ref, which, m).start()

        if toward:
            pl.when(sends[toward])(start)
        else:
            start()

    def halo(ref, which):
        for toward in (-1, 1, 0):
            halo_send(ref, which, toward)

    def halo_wait(ref, which, toward, sent=False):
        picked = [m for m in range(len(MOVES)) if MOVES[m][0] == toward]

        def wait():
            for m in picked:
                copy = halo_copy(ref, which, m)
                if sent:
                    copy.wait_send()
                else:
                    copy.wait_recv()

        if toward:
            pl.when((sends if sent else gets)[toward])(wait)
        else:
            wait()

    pieces = local_sem.shape[0] - 1
    chunk = slots // pieces
    jac_copies = [
        pltpu.make_async_copy(
            jac_in.at[q * chunk:(q + 1) * chunk], jac.at[q * chunk:(q + 1) * chunk], local_sem.at[q]
        )
        for q in range(pieces)
    ]
    kap_copy = pltpu.make_async_copy(
        kh_in, kap.at[MOST:MOST + cells_i, SIDE:SIDE + cells_j, :], local_sem.at[pieces]
    )
    kap_copy.start()
    for copy in jac_copies:
        copy.start()

    partners = [(lat_of(i), lon_of(j)) for i, j in MOVES if i and j]
    partners += [(lat_of(d), b) for d in range(1, n_lat)]
    partners += [(a, lon_of(d)) for d in range(1, n_lon)]
    barrier = pltpu.get_barrier_semaphore()
    for to_lat, to_lon in partners:
        pl.semaphore_signal(
            barrier, inc=1, device_id=(to_lat, to_lon), device_id_type=pl.DeviceIdType.MESH
        )

    @pl.when(a == 0)
    def _():
        kap[0:MOST] = jnp.zeros((MOST, span, levels), F32)
        for field in range(5):
            ext[field, 0:MOST] = jnp.zeros((MOST, span, levels), F32)

    @pl.when(a == n_lat - 1)
    def _():
        kap[MOST + cells_i:] = jnp.zeros((MOST, span, levels), F32)
        for field in range(5):
            ext[field, MOST + cells_i:] = jnp.zeros((MOST, span, levels), F32)

    def packed(value):
        square[0:obs, 0:obs] = value
        turned = jnp.transpose(square[...])[0:obs, 0:obs]
        return jnp.concatenate([turned[0:half], turned[half:obs]], axis=1)

    square[...] = jnp.zeros(square.shape, F32)
    wown[...] = packed(weight[...])
    band[0, core, chip] = wown[...] * packed(innov[...])

    pl.semaphore_wait(barrier, len(partners))
    kap_copy.wait()
    order = sorted(range(1, chips), key=lambda d: -min(d, chips - d))

    def send_band(r):
        mine = band.at[r, core, chip]
        sent = {
            d: remote(mine, mine, ag_s.at[r, d], ag_r.at[r, d], a, chip_of(d) * 2 + core)
            for d in order
        }
        return sent, [remote(mine, mine, fw_s.at[r, 0], fw_r.at[r, 0], a, sibling)]

    def wait_band(r, sent, forwards):
        for d in reversed(order):
            sent[d].wait_recv()
            arrived = band.at[r, core, chip_of(-d)]
            forwards.append(remote(arrived, arrived, fw_s.at[r, d], fw_r.at[r, d], a, sibling))
        for copy in forwards:
            copy.wait_recv()

    gathering = send_band(0)
    halo(kap, 0)

    lst[...] = jnp.full(lst.shape, n_lon * obs, jnp.int32)
    lst[0:2, 0:slots] = rows_in[...]
    padded = lst.shape[1]
    row_line = lst[0:1, :]
    col_line = lst[1:2, :]

    def upright(line):
        return jnp.transpose(jnp.broadcast_to(line.astype(F32), (128, padded))).astype(jnp.int32)

    def hot(test):
        return jnp.where(test, 1.0, 0.0).astype(BF16)

    lane = lax.broadcasted_iota(jnp.int32, (padded, 128), 1)
    sub = lax.broadcasted_iota(jnp.int32, (128, padded), 0)
    row_column = upright(row_line)
    col_column = upright(col_line)
    for j in range(2):
        for q in range(n_lon * half // 128):
            place = slice(128 * q, 128 * q + 128)
            rsel[j, :, place] = hot(row_column == 256 * q + half * j + obs * (lane // half) + lane % half)
            rselt[j, place, :] = hot(row_line == 256 * q + half * j + obs * (sub // half) + sub % half)
    for q in range(columns // 128):
        place = slice(128 * q, 128 * q + 128)
        chot[place, :] = hot((col_line == sub + 128 * q) & (row_line < n_lon * obs))
        chott[:, place] = hot(col_column == lane + 128 * q)
    contrib[slots:padded, :] = jnp.zeros((padded - slots, levels), F32)
    observed[slots:padded, :] = jnp.zeros((padded - slots, 128), F32)

    for q, copy in enumerate(jac_copies):
        copy.wait()

        @pl.loop(q * chunk // 4, (q + 1) * chunk // 4)
        def _(g):
            block = jac[pl.ds(4 * g, 4)].reshape(4 * obs, levels)
            place = pl.ds(pl.multiple_of(4 * obs * g, 4 * obs), 4 * obs)
            turned = pl.ds(pl.multiple_of(levels * g, levels), levels)
            jparts[0, place, :], jparts[1, place, :] = split(block)
            jturn[0, turned, :], jturn[1, turned, :] = split(jnp.transpose(block))

    level = lax.broadcasted_iota(jnp.int32, (cells_j, levels), 1)

    @pl.loop(0, cells_i)
    def _(i):
        root = jnp.sqrt(kv[i])
        below = jnp.where(level < levels - 1, root * pltpu.roll(root, levels - 1, 1), 0.0)
        above = jnp.where(level > 0, root * pltpu.roll(root, 1, 1), 0.0)
        vco[0, i] = 1.0 - below - above
        vco[1, i] = below
        vco[2, i] = above

    lateral_count = jnp.full((span, levels), counts[0], jnp.int32)
    vertical_count = jnp.full((cells_j, levels), counts[1], jnp.int32)

    def vertical(rows, values):
        for p in range(MOST):
            news = [
                vco[0, i] * w + vco[1, i] * pltpu.roll(w, levels - 1, 1) + vco[2, i] * pltpu.roll(w, 1, 1)
                for i, w in zip(rows, values)
            ]
            values = news if p < LEAST else [
                jnp.where(vertical_count > p, new, w) for new, w in zip(news, values)
            ]
        return values

    def lateral(field, target):
        def rows_of(p, rows):
            source = ext.at[field] if p == 0 else tmp.at[p - 1]
            news = []
            for i in rows:
                w = source[i]
                new = (
                    lco[0, i] * w + lco[1, i] * source[i - 1] + lco[2, i] * source[i + 1]
                    + lco[3, i] * pltpu.roll(w, 1, 0) + lco[4, i] * pltpu.roll(w, span - 1, 0)
                )
                news.append(new if p < LEAST else jnp.where(lateral_count > p, new, w))
            for i, new in zip(rows, news):
                if p < MOST - 1:
                    tmp[p, i] = new
                else:
                    place = (i - MOST) * cells_j
                    if not isinstance(place, int):
                        place = pl.multiple_of(place, cells_j)
                    target[pl.ds(place, cells_j), :] = new[SIDE:SIDE + cells_j, :]

        halo_wait(ext.at[field], field + 1, 0)
        for p in range(MOST):
            first = MOST + p + 1

            @pl.loop(0, (cells_i - 2 * p - 2) // 2)
            def _(g, p=p, first=first):
                rows_of(p, [first + 2 * g, first + 2 * g + 1])

        halo_wait(ext.at[field], field + 1, -1)
        halo_wait(ext.at[field], field + 1, 1)
        for p in range(MOST):
            top = p + 1
            low = MOST + cells_i - p - 1

            @pl.loop(0, MOST // 2)
            def _(g, p=p, top=top, low=low):
                rows_of(p, [top + 2 * g, top + 2 * g + 1, low + 2 * g, low + 2 * g + 1])

    def send_sum(i, tile, along_lat):
        sum_out[i] = tile
        count = n_lat if along_lat else n_lon
        return [
            remote(
                sum_out.at[i], sum_in.at[i, d - 1], sum_s.at[i, d - 1], sum_r.at[i, d - 1],
                lat_of(d) if along_lat else a, b if along_lat else lon_of(d),
            )
            for d in range(1, count)
        ]

    def take_sum(i, copies):
        for copy in copies:
            copy.wait_recv()
        tile = sum_out[i]
        for d in range(len(copies)):
            tile = tile + sum_in[i, d]
        return tile

    side8 = lax.broadcasted_iota(jnp.int32, (padded, 128), 0)
    lane8 = lax.broadcasted_iota(jnp.int32, (padded, 128), 1)
    quarter = side8 % 4
    left_block = lane8 // obs == quarter
    right_block = lane8 // obs + 2 == quarter
    first_half = side8 % 8 < 4
    low_lanes = lane8 < obs

    def put_lhs(part, left, right):
        lhs[part, :, 0:128] = left[0:slots]
        lhs[part, :, 128:256] = right[0:slots]

    def natural(part, g):
        first = 8 * obs * g
        return jnp.concatenate(
            [jparts[part, first:first + 4 * obs, :], jparts[part, first + 4 * obs:first + 8 * obs, :]],
            axis=1,
        )

    def turned(part, g):
        return jturn[part, 2 * levels * g:2 * levels * (g + 1), :]

    def products(matrix, finish):
        for g in range(slots // 8):
            place = slice(8 * g, 8 * g + 8)
            left = jnp.concatenate([lhs[0, place, :], lhs[1, place, :]], axis=0).astype(BF16)
            out = sum(jnp.dot(left, matrix(part, g), preferred_element_type=F32) for part in range(2))
            finish(place, out[0:8] + out[8:16])

    def adjoint(r, field):
        values = jnp.concatenate(
            [band[r, k, c] for c in range(chips) for k in range(2)], axis=0
        )
        picked = [pick(rsel[j], values) for j in range(2)]
        for part in range(2):
            taken = jnp.where(low_lanes, picked[0][part], picked[1][part])
            taken = taken + pltpu.roll(taken, obs, 1)
            put_lhs(part, jnp.where(left_block, taken, 0.0), jnp.where(right_block, taken, 0.0))

        def finish(place, out):
            contrib[place, :] = jnp.where(first_half[0:8], out[:, 0:128], out[:, 128:256])

        products(natural, finish)
        high, low = pick(chot[...], contrib[...])
        cells = high + low
        for i in range(cells_i):
            ext[field, MOST + i, SIDE:SIDE + cells_j, :] = cells[cells_j * i:cells_j * i + cells_j, :]

    def observe(which, r):
        picked = pick(chott[...], evolved[which])
        for part in range(2):
            put_lhs(part, jnp.where(first_half, picked[part], 0.0), jnp.where(first_half, 0.0, picked[part]))

        def finish(place, out):
            value = jnp.where(left_block[0:8], out[:, 0:128], 0.0) + jnp.where(
                right_block[0:8], out[:, 128:256], 0.0
            )
            observed[place, :] = value + pltpu.roll(value, obs, 1)

        products(turned, finish)
        high, low = zip(*(pick(rselt[j], observed[...]) for j in range(2)))
        narrow = lax.broadcasted_iota(jnp.int32, high[0].shape, 1) < obs
        partial = jnp.where(narrow, high[0] + low[0], high[1] + low[1])
        for c in range(chips):
            for k in range(2):
                first = half * (2 * c + k)
                zbuf[r, k, c] = partial[first:first + half, :]
        remote(zbuf.at[r, 1 - core], zsib.at[r], sib_s.at[r], sib_r.at[r], a, sibling).wait_recv()
        for c in range(chips):
            zchip[r, c] = zbuf[r, core, c] + zsib[r, c]
        copies = [
            remote(
                zchip.at[r, chip_of(d)], zin.at[r, d - 1], rs_s.at[r, d - 1], rs_r.at[r, d - 1],
                a, chip_of(d) * 2 + core,
            )
            for d in order
        ]
        total = zchip[r, chip]
        for copy in copies:
            copy.wait_recv()
        for d in range(1, chips):
            total = total + zin[r, d - 1]
        return total

    def fold(value):
        return jnp.sum(value.reshape(value.shape[0] // 8, 8, levels), axis=0)

    def whole(value):
        return jnp.sum(jnp.sum(value, axis=0, keepdims=True), axis=1, keepdims=True)

    def two_rows(first, second):
        sub8 = lax.broadcasted_iota(jnp.int32, (8, levels), 0)
        return jnp.where(
            sub8 == 0,
            jnp.sum(first, axis=0, keepdims=True),
            jnp.where(sub8 == 1, jnp.sum(second, axis=0, keepdims=True), 0.0),
        )

    wait_band(0, *gathering)
    adjoint(0, 0)
    halo(ext.at[0], 1)

    for toward in (-1, 0, 1):
        halo_wait(kap, 0, toward)

    @pl.loop(0, total_rows // 2)
    def _(g):
        for u in range(2):
            tmp[0, 2 * g + u] = jnp.sqrt(kap[2 * g + u])

    @pl.loop(0, total_rows // 2 - 1)
    def _(g):
        for u in range(2):
            i = 2 * g + 1 + u
            root = tmp[0, i]
            up = root * tmp[0, i - 1]
            down = root * tmp[0, i + 1]
            west = root * pltpu.roll(root, 1, 0)
            east = root * pltpu.roll(root, span - 1, 0)
            lco[0, i] = 1.0 - (up + down + west + east)
            lco[1, i] = up
            lco[2, i] = down
            lco[3, i] = west
            lco[4, i] = east

    def row(ref, i):
        return ref[i * cells_j:(i + 1) * cells_j, :]

    def middle(field, i, value):
        ext[field, MOST + i, SIDE:SIDE + cells_j, :] = value

    GROUP = 8
    groups = [list(range(q, q + GROUP)) for q in range(0, cells_i, GROUP)]

    def spread_and_send(field, work):
        accs = None
        for q, rows in enumerate(groups):
            parts = work(rows)
            accs = parts if accs is None else [x + y for x, y in zip(accs, parts)]
            if q == 0:
                halo_send(ext.at[field], field + 1, -1)
        halo_send(ext.at[field], field + 1, 1)
        halo_send(ext.at[field], field + 1, 0)
        return accs

    lateral(0, done)

    def gradient_rows(rows):
        ws = vertical(rows, [row(done, i) for i in rows])
        total = sum(fold(w * w) for w in ws)
        nexts = vertical(rows, ws)
        for i, w, following in zip(rows, ws, nexts):
            grad[i] = w
            middle(1, i, following)
        return [total]

    (total,) = spread_and_send(1, gradient_rows)
    norm_lat = send_sum(0, total, True)
    lateral(1, evolved.at[0])
    norm_lon = send_sum(1, take_sum(0, norm_lat), False)

    piece = observe(0, 0)
    zown[...] = piece
    weighted = wown[...] * piece
    band[1, core, chip] = weighted
    gathering = send_band(1)
    curve_lat = send_sum(2, fold(weighted * piece), True)
    norm = whole(take_sum(1, norm_lon))
    wait_band(1, *gathering)
    adjoint(1, 2)
    halo(ext.at[2], 3)
    curve_lon = send_sum(3, take_sum(2, curve_lat), False)
    lateral(2, done)
    alpha_first = norm / (norm + whole(take_sum(3, curve_lon)))
    alpha_wide = jnp.broadcast_to(alpha_first, (cells_j, levels))

    def residual_rows(rows):
        ws = vertical(rows, [row(done, i) for i in rows])
        gs = [grad[i] for i in rows]
        news = [g - alpha_wide * (g + w) for g, w in zip(gs, ws)]
        squares = sum(fold(new * new) for new in news)
        crosses = sum(fold(new * g) for new, g in zip(news, gs))
        nexts = vertical(rows, news)
        for i, new, following in zip(rows, news, nexts):
            resid[i] = new
            middle(3, i, following)
        return [squares, crosses]

    squares, crosses = spread_and_send(3, residual_rows)
    norm_lat = send_sum(4, two_rows(squares, crosses), True)
    lateral(3, evolved.at[1])
    norm_lon = send_sum(5, take_sum(4, norm_lat), False)

    piece = observe(1, 1)
    tile = take_sum(5, norm_lon)
    norm_next = jnp.sum(tile[0:1, :], axis=1, keepdims=True)
    cross = jnp.sum(tile[1:2, :], axis=1, keepdims=True)
    beta = norm_next / norm
    self_product = norm_next + 2.0 * beta * cross + beta * beta * norm
    piece = piece + beta * zown[...]
    weighted = wown[...] * piece
    band[2, core, chip] = weighted
    gathering = send_band(2)
    curve_lat = send_sum(6, fold(weighted * piece), True)
    wait_band(2, *gathering)
    adjoint(2, 4)
    halo(ext.at[4], 5)
    curve_lon = send_sum(7, take_sum(6, curve_lat), False)
    lateral(4, done)
    alpha_second = norm_next / (self_product + whole(take_sum(7, curve_lon)))
    second_wide = jnp.broadcast_to(alpha_second, (cells_j, levels))
    beta_wide = jnp.broadcast_to(beta, (cells_j, levels))
    for rows in groups:
        ws = vertical(rows, [row(done, i) for i in rows])
        for i, w in zip(rows, ws):
            r = resid[i]
            residual_out[i] = r - second_wide * (r + beta_wide * grad[i] + w)
            first, second = row(evolved.at[0], i), row(evolved.at[1], i)
            increment[i] = alpha_wide * first + second_wide * (second + beta_wide * first)

    for copy in started:
        copy.wait_send()
    for which in range(6):
        ref = kap if which == 0 else ext.at[which - 1]
        for toward in (-1, 0, 1):
            halo_wait(ref, which, toward, sent=True)


def local(n_lat, n_lon, innovation, obs_weight, jacobian, block_list, pass_counts, kappa_h, kappa_v):
    cells_i, cells_j, levels = kappa_h.shape
    slots, obs, _ = jacobian.shape
    shape = (n_lat, n_lon, cells_i, cells_j, levels, slots, obs)
    chips = n_lon // 2
    half = obs // 2
    span = cells_j + 2 * SIDE
    total_rows = cells_i + 2 * MOST
    padded = -(-slots // 128) * 128
    columns = cells_i * cells_j
    peers = max(n_lat, n_lon) - 1
    vmem = pltpu.VMEM
    dma = pltpu.SemaphoreType.DMA
    field = jax.ShapeDtypeStruct((cells_i, cells_j, levels), F32)
    in_vmem = pl.BlockSpec(memory_space=pltpu.VMEM)
    in_smem = pl.BlockSpec(memory_space=pltpu.SMEM)
    in_any = pl.BlockSpec(memory_space=pl.ANY)
    return pl.pallas_call(
        functools.partial(kernel, shape),
        out_shape=(field, field),
        in_specs=[in_smem, in_vmem, in_vmem, in_vmem, in_any, in_any, in_vmem],
        out_specs=(in_vmem, in_vmem),
        scratch_shapes=[
            vmem((slots, obs, levels), F32),
            vmem((2, slots * obs, levels), BF16),
            vmem((2, slots // 4 * levels, 4 * obs), BF16),
            vmem((total_rows, span, levels), F32),
            vmem((5, total_rows, span, levels), F32),
            vmem((MOST - 1, total_rows, span, levels), F32),
            vmem((5, total_rows, span, levels), F32),
            vmem((3, cells_i, cells_j, levels), F32),
            vmem((8, padded), jnp.int32),
            vmem((2, padded, half * n_lon), BF16),
            vmem((2, half * n_lon, padded), BF16),
            vmem((columns, padded), BF16),
            vmem((padded, columns), BF16),
            vmem((2, slots, 256), F32),
            vmem((padded, levels), F32),
            vmem((padded, 128), F32),
            vmem((columns, levels), F32),
            vmem((cells_i, cells_j, levels), F32),
            vmem((cells_i, cells_j, levels), F32),
            vmem((2, columns, levels), F32),
            vmem((128, 128), F32),
            vmem((2, 2, chips, half, 128), F32),
            vmem((2, chips, half, 128), F32),
            vmem((2, chips, half, 128), F32),
            vmem((2, chips - 1, half, 128), F32),
            vmem((half, 128), F32),
            vmem((half, 128), F32),
            vmem((3, 2, chips, half, 128), F32),
            vmem((8, 8, 128), F32),
            vmem((8, peers, 8, 128), F32),
            dma((5,)),
            dma((6, 8)), dma((6, 8)),
            dma((2,)), dma((2,)),
            dma((2, chips - 1)), dma((2, chips - 1)),
            dma((3, chips)), dma((3, chips)),
            dma((3, chips)), dma((3, chips)),
            dma((8, peers)), dma((8, peers)),
        ],
        compiler_params=pltpu.CompilerParams(
            collective_id=0, has_side_effects=True, vmem_limit_bytes=60 * 1024 * 1024
        ),
    )(pass_counts, block_list, innovation, obs_weight, jacobian, kappa_h, kappa_v)


def solution(mesh):
    return jax.shard_map(
        functools.partial(local, mesh.shape["lat"], mesh.shape["lon"]),
        mesh=mesh,
        in_specs=(
            P(None, ("lat", "lon")),
            P(None, ("lat", "lon")),
            P(("lat", "lon"), None, None),
            P(None, ("lat", "lon")),
            P(),
            P("lat", "lon", None),
            P("lat", "lon", None),
        ),
        out_specs=(P("lat", "lon", None), P("lat", "lon", None)),
        check_vma=False,
    )
```

```python
import functools

import jax
import jax.numpy as jnp
from jax import lax
from jax.experimental import pallas as pl
from jax.experimental.pallas import tpu as pltpu
from jax.sharding import PartitionSpec as P

MOST = 6
LEAST = 3
SIDE = 8
F32 = jnp.float32
BF16 = jnp.bfloat16
MOVES = tuple((i, j) for i in (-1, 0, 1) for j in (-1, 0, 1) if (i, j) != (0, 0))


def split(value):
    high = value.astype(BF16)
    return high, (value - high.astype(F32)).astype(BF16)


def pick(table, value):
    both = jnp.concatenate(split(value), axis=1)
    out = jnp.dot(table, both, preferred_element_type=F32)
    width = value.shape[1]
    return out[:, :width], out[:, width:]


def kernel(
    shape, counts, rows_hbm, innov_hbm, weight_hbm, jac_in, kh_in, kv_hbm,
    increment, residual_out,
    rows_in, innov, weight, kv, jac, jparts, jturn, kap, ext, tmp, lco, vco, lst, rsel, rselt, chot, chott, lhs, contrib, observed,
    done, grad, resid, turn_in, turn_out, evolved, square,
    zbuf, zsib, zchip, zin, zown, wown, band, sum_out, sum_in,
    local_sem, halo_s, halo_r, sib_s, sib_r, rs_s, rs_r,
    ag_s, ag_r, fw_s, fw_r, sum_s, sum_r,
):
    n_lat, n_lon, cells_i, cells_j, levels, slots, obs = shape
    chips = n_lon // 2
    half = obs // 2
    span = cells_j + 2 * SIDE
    total_rows = cells_i + 2 * MOST
    columns = cells_i * cells_j
    a = lax.axis_index("lat")
    b = lax.axis_index("lon")
    chip = b // 2
    core = lax.rem(b, 2)
    sibling = chip * 2 + 1 - core
    lat_of = lambda d: lax.rem(a + d + n_lat, n_lat)
    lon_of = lambda d: lax.rem(b + d + n_lon, n_lon)
    chip_of = lambda d: lax.rem(chip + d + chips, chips)
    started = []

    def describe(src, dst, ss, rs, to_lat, to_lon):
        return pltpu.make_async_remote_copy(
            src_ref=src, dst_ref=dst, send_sem=ss, recv_sem=rs,
            device_id=(to_lat, to_lon), device_id_type=pl.DeviceIdType.MESH,
        )

    def remote(*args):
        copy = describe(*args)
        copy.start()
        started.append(copy)
        return copy

    rows_src = {-1: slice(MOST, 2 * MOST), 0: slice(MOST, MOST + cells_i), 1: slice(cells_i, cells_i + MOST)}
    rows_dst = {-1: slice(MOST + cells_i, total_rows), 0: slice(MOST, MOST + cells_i), 1: slice(0, MOST)}
    cols_src = {-1: slice(SIDE, 2 * SIDE), 0: slice(SIDE, SIDE + cells_j), 1: slice(cells_j, cells_j + SIDE)}
    cols_dst = {-1: slice(SIDE + cells_j, span), 0: slice(SIDE, SIDE + cells_j), 1: slice(0, SIDE)}
    sends = {-1: a > 0, 1: a < n_lat - 1}
    gets = {-1: a < n_lat - 1, 1: a > 0}

    def halo_copy(ref, which, m):
        i, j = MOVES[m]
        return describe(
            ref.at[rows_src[i], cols_src[j], :], ref.at[rows_dst[i], cols_dst[j], :],
            halo_s.at[which, m], halo_r.at[which, m], lat_of(i), lon_of(j),
        )

    def halo_send(ref, which, toward):
        picked = [m for m in range(len(MOVES)) if MOVES[m][0] == toward]
        picked.sort(key=lambda m: MOVES[m][1] == 0)

        def start():
            for m in picked:
                halo_copy(ref, which, m).start()

        if toward:
            pl.when(sends[toward])(start)
        else:
            start()

    def halo(ref, which):
        for toward in (-1, 1, 0):
            halo_send(ref, which, toward)

    def halo_wait(ref, which, toward, sent=False):
        picked = [m for m in range(len(MOVES)) if MOVES[m][0] == toward]

        def wait():
            for m in picked:
                copy = halo_copy(ref, which, m)
                if sent:
                    copy.wait_send()
                else:
                    copy.wait_recv()

        if toward:
            pl.when((sends if sent else gets)[toward])(wait)
        else:
            wait()

    pieces = 4
    chunk = slots // pieces
    jac_copies = [
        pltpu.make_async_copy(
            jac_in.at[q * chunk:(q + 1) * chunk], jac.at[q * chunk:(q + 1) * chunk], local_sem.at[q]
        )
        for q in range(pieces)
    ]
    kap_copy = pltpu.make_async_copy(
        kh_in, kap.at[MOST:MOST + cells_i, SIDE:SIDE + cells_j, :], local_sem.at[pieces]
    )
    small_copies = [
        pltpu.make_async_copy(src, dst, local_sem.at[pieces + 1 + q])
        for q, (src, dst) in enumerate(
            ((rows_hbm, rows_in), (innov_hbm, innov), (weight_hbm, weight), (kv_hbm, kv))
        )
    ]
    for copy in small_copies:
        copy.start()
    kap_copy.start()
    for copy in jac_copies:
        copy.start()

    partners = [(lat_of(i), lon_of(j)) for i, j in MOVES if i and j]
    partners += [(lat_of(d), b) for d in range(1, n_lat)]
    partners += [(a, lon_of(d)) for d in range(1, n_lon)]
    barrier = pltpu.get_barrier_semaphore()
    for to_lat, to_lon in partners:
        pl.semaphore_signal(
            barrier, inc=1, device_id=(to_lat, to_lon), device_id_type=pl.DeviceIdType.MESH
        )

    @pl.when(a == 0)
    def _():
        kap[0:MOST] = jnp.zeros((MOST, span, levels), F32)
        for field in range(5):
            ext[field, 0:MOST] = jnp.zeros((MOST, span, levels), F32)

    @pl.when(a == n_lat - 1)
    def _():
        kap[MOST + cells_i:] = jnp.zeros((MOST, span, levels), F32)
        for field in range(5):
            ext[field, MOST + cells_i:] = jnp.zeros((MOST, span, levels), F32)

    def packed(value):
        square[0:obs, 0:obs] = value
        turned = jnp.transpose(square[...])[0:obs, 0:obs]
        return jnp.concatenate([turned[0:half], turned[half:obs]], axis=1)

    square[...] = jnp.zeros(square.shape, F32)
    for copy in small_copies:
        copy.wait()
    wown[...] = packed(weight[...])
    band[0, core, chip] = wown[...] * packed(innov[...])

    pl.semaphore_wait(barrier, len(partners))
    kap_copy.wait()
    order = sorted(range(1, chips), key=lambda d: -min(d, chips - d))

    def send_band(r):
        mine = band.at[r, core, chip]
        sent = {
            d: remote(mine, mine, ag_s.at[r, d], ag_r.at[r, d], a, chip_of(d) * 2 + core)
            for d in order
        }
        return sent, [remote(mine, mine, fw_s.at[r, 0], fw_r.at[r, 0], a, sibling)]

    def forward_band(r, sent, forwards):
        for d in reversed(order):
            sent[d].wait_recv()
            arrived = band.at[r, core, chip_of(-d)]
            forwards.append(remote(arrived, arrived, fw_s.at[r, d], fw_r.at[r, d], a, sibling))
        return forwards

    def wait_band(forwards):
        for copy in forwards:
            copy.wait_recv()

    gathering = send_band(0)
    halo(kap, 0)

    lst[...] = jnp.full(lst.shape, n_lon * obs, jnp.int32)
    lst[0:2, 0:slots] = rows_in[...]
    padded = lst.shape[1]
    row_line = lst[0:1, :]
    col_line = lst[1:2, :]

    def upright(line):
        return jnp.transpose(jnp.broadcast_to(line.astype(F32), (128, padded))).astype(jnp.int32)

    def hot(test):
        return jnp.where(test, 1.0, 0.0).astype(BF16)

    lane = lax.broadcasted_iota(jnp.int32, (padded, 128), 1)
    sub = lax.broadcasted_iota(jnp.int32, (128, padded), 0)
    row_column = upright(row_line)
    col_column = upright(col_line)
    for j in range(2):
        for q in range(n_lon * half // 128):
            place = slice(128 * q, 128 * q + 128)
            rsel[j, :, place] = hot(row_column == 256 * q + half * j + obs * (lane // half) + lane % half)
            rselt[j, place, :] = hot(row_line == 256 * q + half * j + obs * (sub // half) + sub % half)
    for q in range(columns // 128):
        place = slice(128 * q, 128 * q + 128)
        chot[place, :] = hot((col_line == sub + 128 * q) & (row_line < n_lon * obs))
        chott[:, place] = hot(col_column == lane + 128 * q)
    contrib[slots:padded, :] = jnp.zeros((padded - slots, levels), F32)
    observed[slots:padded, :] = jnp.zeros((padded - slots, 128), F32)

    STEPS = levels // 8
    blocks = columns // 128

    def upended(q, value):
        turn_in[128 * q:128 * q + 128, :] = jnp.transpose(value)
        return [turn_in[pl.ds(128 * q + j, 8, stride=STEPS), :] for j in range(STEPS)]

    def restored(q, parts):
        for j in range(STEPS):
            turn_out[pl.ds(128 * q + j, 8, stride=STEPS), :] = parts[j]
        return jnp.transpose(turn_out[128 * q:128 * q + 128, :])

    def keep_parts(ref, q, parts):
        for j in range(STEPS):
            ref[128 * q + 8 * j:128 * q + 8 * j + 8, :] = parts[j]

    def kept(ref, q):
        return [ref[128 * q + 8 * j:128 * q + 8 * j + 8, :] for j in range(STEPS)]

    sublane = lax.broadcasted_iota(jnp.int32, (8, 128), 0)
    rows_each = 128 // cells_j
    for q in range(blocks):
        roots = [
            jnp.sqrt(part)
            for part in upended(q, kv[rows_each * q:rows_each * (q + 1)].reshape(128, levels))
        ]
        nexts = roots[1:] + [jnp.where(sublane < 7, pltpu.roll(roots[0], 7, 0), 0.0)]
        keep_parts(vco, q, [root * following for root, following in zip(roots, nexts)])

    forwards = None
    for q, copy in enumerate(jac_copies):
        if q == pieces - 1:
            forwards = forward_band(0, *gathering)
        copy.wait()

        @pl.loop(q * chunk // 4, (q + 1) * chunk // 4)
        def _(g):
            block = jac[pl.ds(4 * g, 4)].reshape(4 * obs, levels)
            place = pl.ds(pl.multiple_of(4 * obs * g, 4 * obs), 4 * obs)
            turned = pl.ds(pl.multiple_of(levels * g, levels), levels)
            jparts[0, place, :], jparts[1, place, :] = split(block)
            jturn[0, turned, :], jturn[1, turned, :] = split(jnp.transpose(block))


    lateral_count = jnp.full((span, levels), counts[0], jnp.int32)
    vertical_count = jnp.full((8, 128), counts[1], jnp.int32)

    def vertical(q, parts):
        for p in range(MOST):
            faces = kept(vco, q)
            uppers = parts[1:] + [pltpu.roll(parts[0], 7, 0)]
            flows = [face * (upper - w) for face, upper, w in zip(faces, uppers, parts)]
            lowers = [pltpu.roll(flows[-1], 1, 0)] + flows[:-1]
            news = [w + (flow - lower) for w, flow, lower in zip(parts, flows, lowers)]
            parts = news if p < LEAST else [
                jnp.where(vertical_count > p, new, w) for new, w in zip(news, parts)
            ]
        return parts

    def lateral(field, target, meanwhile=lambda: None):
        def rows_of(p, first, count):
            source = ext.at[field] if p == 0 else tmp.at[p - 1]
            ws = [source[first + q] for q in range(-1, count + 1)]
            flows = [lco[0, first + q - 1] * (ws[q + 1] - ws[q]) for q in range(count + 1)]
            news = []
            for q in range(count):
                w = ws[q + 1]
                east = lco[1, first + q] * (pltpu.roll(w, span - 1, 0) - w)
                new = w + (flows[q + 1] - flows[q]) + (east - pltpu.roll(east, 1, 0))
                news.append(new if p < LEAST else jnp.where(lateral_count > p, new, w))
            for q, new in enumerate(news):
                i = first + q
                if p < MOST - 1:
                    tmp[p, i] = new
                else:
                    place = (i - MOST) * cells_j
                    if not isinstance(place, int):
                        place = pl.multiple_of(place, cells_j)
                    target[pl.ds(place, cells_j), :] = new[SIDE:SIDE + cells_j, :]

        halo_wait(ext.at[field], field + 1, 0)
        for p in range(MOST):
            first = MOST + p + 1
            count = cells_i // 2 - p - 1

            @pl.loop(0, 2)
            def _(g, p=p, first=first, count=count):
                rows_of(p, first + count * g, count)

        halo_wait(ext.at[field], field + 1, -1)
        halo_wait(ext.at[field], field + 1, 1)
        for p in range(MOST):
            top = p + 1
            low = MOST + cells_i - p - 1

            @pl.loop(0, 2)
            def _(g, p=p, top=top, low=low):
                rows_of(p, top + (low - top) * g, MOST)

        return meanwhile()

    def send_sum(i, tile, along_lat):
        sum_out[i] = tile
        count = n_lat if along_lat else n_lon
        return [
            remote(
                sum_out.at[i], sum_in.at[i, d - 1], sum_s.at[i, d - 1], sum_r.at[i, d - 1],
                lat_of(d) if along_lat else a, b if along_lat else lon_of(d),
            )
            for d in range(1, count)
        ]

    def take_sum(i, copies):
        for copy in copies:
            copy.wait_recv()
        tile = sum_out[i]
        for d in range(len(copies)):
            tile = tile + sum_in[i, d]
        return tile

    side8 = lax.broadcasted_iota(jnp.int32, (padded, 128), 0)
    lane8 = lax.broadcasted_iota(jnp.int32, (padded, 128), 1)
    quarter = side8 % 4
    left_block = lane8 // obs == quarter
    right_block = lane8 // obs + 2 == quarter
    first_half = side8 % 8 < 4
    low_lanes = lane8 < obs

    def put_lhs(part, left, right):
        lhs[part, :, 0:128] = left[0:slots]
        lhs[part, :, 128:256] = right[0:slots]

    def natural(part, g):
        first = 8 * obs * g
        return jnp.concatenate(
            [jparts[part, first:first + 4 * obs, :], jparts[part, first + 4 * obs:first + 8 * obs, :]],
            axis=1,
        )

    def turned(part, g):
        return jturn[part, 2 * levels * g:2 * levels * (g + 1), :]

    def products(matrix, finish):
        for g in range(slots // 8):
            place = slice(8 * g, 8 * g + 8)
            left = jnp.concatenate([lhs[0, place, :], lhs[1, place, :]], axis=0).astype(BF16)
            out = sum(jnp.dot(left, matrix(part, g), preferred_element_type=F32) for part in range(2))
            finish(place, out[0:8] + out[8:16])

    def adjoint(r, field):
        values = jnp.concatenate(
            [band[r, k, c] for c in range(chips) for k in range(2)], axis=0
        )
        picked = [pick(rsel[j], values) for j in range(2)]
        for part in range(2):
            taken = jnp.where(low_lanes, picked[0][part], picked[1][part])
            taken = taken + pltpu.roll(taken, obs, 1)
            put_lhs(part, jnp.where(left_block, taken, 0.0), jnp.where(right_block, taken, 0.0))

        def finish(place, out):
            contrib[place, :] = jnp.where(first_half[0:8], out[:, 0:128], out[:, 128:256])

        products(natural, finish)
        high, low = pick(chot[...], contrib[...])
        cells = high + low
        for i in range(cells_i):
            ext[field, MOST + i, SIDE:SIDE + cells_j, :] = cells[cells_j * i:cells_j * i + cells_j, :]

    def observe(which, r):
        picked = pick(chott[...], evolved[which])
        for part in range(2):
            put_lhs(part, jnp.where(first_half, picked[part], 0.0), jnp.where(first_half, 0.0, picked[part]))

        def finish(place, out):
            value = jnp.where(left_block[0:8], out[:, 0:128], 0.0) + jnp.where(
                right_block[0:8], out[:, 128:256], 0.0
            )
            observed[place, :] = value + pltpu.roll(value, obs, 1)

        products(turned, finish)
        high, low = zip(*(pick(rselt[j], observed[...]) for j in range(2)))
        narrow = lax.broadcasted_iota(jnp.int32, high[0].shape, 1) < obs
        partial = jnp.where(narrow, high[0] + low[0], high[1] + low[1])
        for c in range(chips):
            for k in range(2):
                first = half * (2 * c + k)
                zbuf[r, k, c] = partial[first:first + half, :]
        remote(zbuf.at[r, 1 - core], zsib.at[r], sib_s.at[r], sib_r.at[r], a, sibling).wait_recv()
        for c in range(chips):
            zchip[r, c] = zbuf[r, core, c] + zsib[r, c]
        copies = [
            remote(
                zchip.at[r, chip_of(d)], zin.at[r, d - 1], rs_s.at[r, d - 1], rs_r.at[r, d - 1],
                a, chip_of(d) * 2 + core,
            )
            for d in order
        ]
        total = zchip[r, chip]
        for copy in copies:
            copy.wait_recv()
        for d in range(1, chips):
            total = total + zin[r, d - 1]
        return total

    def fold(value):
        return jnp.sum(value.reshape(value.shape[0] // 8, 8, levels), axis=0)

    def whole(value):
        return jnp.sum(jnp.sum(value, axis=0, keepdims=True), axis=1, keepdims=True)

    def two_rows(first, second):
        sub8 = lax.broadcasted_iota(jnp.int32, (8, levels), 0)
        return jnp.where(
            sub8 == 0,
            jnp.sum(first, axis=0, keepdims=True),
            jnp.where(sub8 == 1, jnp.sum(second, axis=0, keepdims=True), 0.0),
        )

    wait_band(forwards)
    adjoint(0, 0)
    halo(ext.at[0], 1)

    for toward in (-1, 0, 1):
        halo_wait(kap, 0, toward)

    @pl.loop(0, total_rows // 2)
    def _(g):
        for u in range(2):
            tmp[0, 2 * g + u] = jnp.sqrt(kap[2 * g + u])

    @pl.loop(0, total_rows // 2)
    def _(g):
        for u in range(2):
            i = 2 * g + u
            root = tmp[0, i]
            lco[0, i] = root * tmp[0, jnp.minimum(i + 1, total_rows - 1)]
            lco[1, i] = root * pltpu.roll(root, span - 1, 0)

    def block_of(ref, q):
        return ref[128 * q:128 * q + 128, :]

    def middle(field, q, value):
        rows = slice(MOST + rows_each * q, MOST + rows_each * (q + 1))
        ext[field, rows, SIDE:SIDE + cells_j, :] = value.reshape(rows_each, cells_j, levels)

    def spread_and_send(field, work):
        accs = None
        for q in range(blocks):
            parts = work(q)
            accs = parts if accs is None else [x + y for x, y in zip(accs, parts)]
            if q == blocks // 2 - 1:
                halo_send(ext.at[field], field + 1, -1)
        halo_send(ext.at[field], field + 1, 1)
        halo_send(ext.at[field], field + 1, 0)
        return accs

    lateral(0, done)

    def gradient_block(q):
        ws = vertical(q, upended(q, block_of(done, q)))
        keep_parts(grad, q, ws)
        middle(1, q, restored(q, vertical(q, ws)))
        return [sum(w * w for w in ws)]

    (total,) = spread_and_send(1, gradient_block)
    norm_lat = send_sum(0, total, True)
    norm_lon = lateral(1, evolved.at[0], lambda: send_sum(1, take_sum(0, norm_lat), False))

    piece = observe(0, 0)
    zown[...] = piece
    weighted = wown[...] * piece
    band[1, core, chip] = weighted
    gathering = send_band(1)
    curve_lat = send_sum(2, fold(weighted * piece), True)
    norm = whole(take_sum(1, norm_lon))
    wait_band(forward_band(1, *gathering))
    adjoint(1, 2)
    halo(ext.at[2], 3)
    curve_lon = send_sum(3, take_sum(2, curve_lat), False)
    lateral(2, done)
    alpha_first = norm / (norm + whole(take_sum(3, curve_lon)))
    alpha_wide = jnp.broadcast_to(alpha_first, (8, 128))

    def residual_block(q):
        ws = vertical(q, upended(q, block_of(done, q)))
        gs = kept(grad, q)
        news = [g - alpha_wide * (g + w) for g, w in zip(gs, ws)]
        keep_parts(resid, q, news)
        middle(3, q, restored(q, vertical(q, news)))
        return [sum(new * new for new in news), sum(new * g for new, g in zip(news, gs))]

    squares, crosses = spread_and_send(3, residual_block)
    norm_lat = send_sum(4, two_rows(squares, crosses), True)
    norm_lon = lateral(3, evolved.at[1], lambda: send_sum(5, take_sum(4, norm_lat), False))

    piece = observe(1, 1)
    tile = take_sum(5, norm_lon)
    norm_next = jnp.sum(tile[0:1, :], axis=1, keepdims=True)
    cross = jnp.sum(tile[1:2, :], axis=1, keepdims=True)
    beta = norm_next / norm
    self_product = norm_next + 2.0 * beta * cross + beta * beta * norm
    piece = piece + beta * zown[...]
    weighted = wown[...] * piece
    band[2, core, chip] = weighted
    gathering = send_band(2)
    curve_lat = send_sum(6, fold(weighted * piece), True)
    wait_band(forward_band(2, *gathering))
    adjoint(2, 4)
    halo(ext.at[4], 5)
    curve_lon = send_sum(7, take_sum(6, curve_lat), False)
    lateral(4, done)
    alpha_second = norm_next / (self_product + whole(take_sum(7, curve_lon)))
    second_wide = jnp.broadcast_to(alpha_second, (8, 128))
    beta_wide = jnp.broadcast_to(beta, (8, 128))
    for q in range(blocks):
        ws = vertical(q, upended(q, block_of(done, q)))
        lasts = [
            r - second_wide * (r + beta_wide * g + w)
            for r, g, w in zip(kept(resid, q), kept(grad, q), ws)
        ]
        rows = slice(rows_each * q, rows_each * (q + 1))
        residual_out[rows] = restored(q, lasts).reshape(rows_each, cells_j, levels)
    for i in range(cells_i):
        first = evolved[0, i * cells_j:(i + 1) * cells_j, :]
        second = evolved[1, i * cells_j:(i + 1) * cells_j, :]
        scale = alpha_first + alpha_second * beta
        increment[i] = scale * first + alpha_second * second

    for copy in started:
        copy.wait_send()
    for which in range(6):
        ref = kap if which == 0 else ext.at[which - 1]
        for toward in (-1, 0, 1):
            halo_wait(ref, which, toward, sent=True)


def hand_over(first, second, first_out, second_out, sems):
    copies = [
        pltpu.make_async_copy(first, first_out, sems.at[0]),
        pltpu.make_async_copy(second, second_out, sems.at[1]),
    ]
    for copy in copies:
        copy.start()
    for copy in copies:
        copy.wait()


def local(n_lat, n_lon, innovation, obs_weight, jacobian, block_list, pass_counts, kappa_h, kappa_v):
    cells_i, cells_j, levels = kappa_h.shape
    slots, obs, _ = jacobian.shape
    shape = (n_lat, n_lon, cells_i, cells_j, levels, slots, obs)
    chips = n_lon // 2
    half = obs // 2
    span = cells_j + 2 * SIDE
    total_rows = cells_i + 2 * MOST
    padded = -(-slots // 128) * 128
    columns = cells_i * cells_j
    peers = max(n_lat, n_lon) - 1
    vmem = pltpu.VMEM
    dma = pltpu.SemaphoreType.DMA
    field = jax.ShapeDtypeStruct((cells_i, cells_j, levels), F32)
    in_vmem = pl.BlockSpec(memory_space=pltpu.VMEM)
    in_smem = pl.BlockSpec(memory_space=pltpu.SMEM)
    in_any = pl.BlockSpec(memory_space=pl.ANY)
    results = pl.pallas_call(
        functools.partial(kernel, shape),
        out_shape=(field, field),
        in_specs=[in_smem] + [in_any] * 6,
        out_specs=(in_vmem, in_vmem),
        scratch_shapes=[
            vmem(block_list.shape, jnp.int32),
            vmem(innovation.shape, F32),
            vmem(obs_weight.shape, F32),
            vmem((cells_i, cells_j, levels), F32),
            vmem((slots, obs, levels), F32),
            vmem((2, slots * obs, levels), BF16),
            vmem((2, slots // 4 * levels, 4 * obs), BF16),
            vmem((total_rows, span, levels), F32),
            vmem((5, total_rows, span, levels), F32),
            vmem((MOST - 1, total_rows, span, levels), F32),
            vmem((2, total_rows, span, levels), F32),
            vmem((columns, levels), F32),
            vmem((8, padded), jnp.int32),
            vmem((2, padded, half * n_lon), BF16),
            vmem((2, half * n_lon, padded), BF16),
            vmem((columns, padded), BF16),
            vmem((padded, columns), BF16),
            vmem((2, slots, 256), F32),
            vmem((padded, levels), F32),
            vmem((padded, 128), F32),
            vmem((columns, levels), F32),
            vmem((columns, levels), F32),
            vmem((columns, levels), F32),
            vmem((columns, levels), F32),
            vmem((columns, levels), F32),
            vmem((2, columns, levels), F32),
            vmem((128, 128), F32),
            vmem((2, 2, chips, half, 128), F32),
            vmem((2, chips, half, 128), F32),
            vmem((2, chips, half, 128), F32),
            vmem((2, chips - 1, half, 128), F32),
            vmem((half, 128), F32),
            vmem((half, 128), F32),
            vmem((3, 2, chips, half, 128), F32),
            vmem((8, 8, 128), F32),
            vmem((8, peers, 8, 128), F32),
            dma((9,)),
            dma((6, 8)), dma((6, 8)),
            dma((2,)), dma((2,)),
            dma((2, chips - 1)), dma((2, chips - 1)),
            dma((3, chips)), dma((3, chips)),
            dma((3, chips)), dma((3, chips)),
            dma((8, peers)), dma((8, peers)),
        ],
        compiler_params=pltpu.CompilerParams(
            collective_id=0, has_side_effects=True, vmem_limit_bytes=60 * 1024 * 1024
        ),
    )(pass_counts, block_list, innovation, obs_weight, jacobian, kappa_h, kappa_v)
    return pl.pallas_call(
        hand_over,
        out_shape=(field, field),
        in_specs=[in_vmem, in_vmem],
        out_specs=(in_any, in_any),
        scratch_shapes=[dma((2,))],
    )(*results)


def solution(mesh):
    return jax.shard_map(
        functools.partial(local, mesh.shape["lat"], mesh.shape["lon"]),
        mesh=mesh,
        in_specs=(
            P(None, ("lat", "lon")),
            P(None, ("lat", "lon")),
            P(("lat", "lon"), None, None),
            P(None, ("lat", "lon")),
            P(),
            P("lat", "lon", None),
            P("lat", "lon", None),
        ),
        out_specs=(P("lat", "lon", None), P("lat", "lon", None)),
        check_vma=False,
    )
```

```python
import functools

import jax
import jax.numpy as jnp
from jax import lax
from jax.experimental import pallas as pl
from jax.experimental.pallas import tpu as pltpu
from jax.sharding import PartitionSpec as P

MOST = 6
LEAST = 3
SIDE = 8
F32 = jnp.float32
BF16 = jnp.bfloat16
MOVES = tuple((i, j) for i in (-1, 0, 1) for j in (-1, 0, 1) if (i, j) != (0, 0))


def split(value):
    high = value.astype(BF16)
    return high, (value - high.astype(F32)).astype(BF16)


def pick(table, value):
    both = jnp.concatenate(split(value), axis=1)
    out = jnp.dot(table, both, preferred_element_type=F32)
    width = value.shape[1]
    return out[:, :width], out[:, width:]


def kernel(
    shape, counts, rows_hbm, innov_hbm, weight_hbm, jac_in, kh_in, kv_hbm,
    increment, residual_out,
    rows_in, innov, weight, kv, jac, jparts, jturn, kap, ext, tmp, lco, vco, lst, rsel, rselt, chot, chott, lhs, contrib, observed,
    done, grad, resid, image, turn_in, turn_out, evolved, square,
    zbuf, zsib, zchip, zin, zown, wown, band, sum_out, sum_in,
    local_sem, halo_s, halo_r, sib_s, sib_r, rs_s, rs_r,
    ag_s, ag_r, fw_s, fw_r, sum_s, sum_r,
):
    n_lat, n_lon, cells_i, cells_j, levels, slots, obs = shape
    chips = n_lon // 2
    half = obs // 2
    span = cells_j + 2 * SIDE
    total_rows = cells_i + 2 * MOST
    columns = cells_i * cells_j
    a = lax.axis_index("lat")
    b = lax.axis_index("lon")
    chip = b // 2
    core = lax.rem(b, 2)
    sibling = chip * 2 + 1 - core
    lat_of = lambda d: lax.rem(a + d + n_lat, n_lat)
    lon_of = lambda d: lax.rem(b + d + n_lon, n_lon)
    chip_of = lambda d: lax.rem(chip + d + chips, chips)
    started = []

    def describe(src, dst, ss, rs, to_lat, to_lon):
        return pltpu.make_async_remote_copy(
            src_ref=src, dst_ref=dst, send_sem=ss, recv_sem=rs,
            device_id=(to_lat, to_lon), device_id_type=pl.DeviceIdType.MESH,
        )

    def remote(*args):
        copy = describe(*args)
        copy.start()
        started.append(copy)
        return copy

    rows_src = {-1: slice(MOST, 2 * MOST), 0: slice(MOST, MOST + cells_i), 1: slice(cells_i, cells_i + MOST)}
    rows_dst = {-1: slice(MOST + cells_i, total_rows), 0: slice(MOST, MOST + cells_i), 1: slice(0, MOST)}
    cols_src = {-1: slice(SIDE, 2 * SIDE), 0: slice(SIDE, SIDE + cells_j), 1: slice(cells_j, cells_j + SIDE)}
    cols_dst = {-1: slice(SIDE + cells_j, span), 0: slice(SIDE, SIDE + cells_j), 1: slice(0, SIDE)}
    sends = {-1: a > 0, 1: a < n_lat - 1}
    gets = {-1: a < n_lat - 1, 1: a > 0}

    def halo_copy(ref, which, m):
        i, j = MOVES[m]
        return describe(
            ref.at[rows_src[i], cols_src[j], :], ref.at[rows_dst[i], cols_dst[j], :],
            halo_s.at[which, m], halo_r.at[which, m], lat_of(i), lon_of(j),
        )

    def halo_send(ref, which, toward):
        picked = [m for m in range(len(MOVES)) if MOVES[m][0] == toward]
        picked.sort(key=lambda m: MOVES[m][1] == 0)

        def start():
            for m in picked:
                halo_copy(ref, which, m).start()

        if toward:
            pl.when(sends[toward])(start)
        else:
            start()

    def halo(ref, which):
        for toward in (-1, 1, 0):
            halo_send(ref, which, toward)

    def halo_wait(ref, which, toward, sent=False):
        picked = [m for m in range(len(MOVES)) if MOVES[m][0] == toward]

        def wait():
            for m in picked:
                copy = halo_copy(ref, which, m)
                if sent:
                    copy.wait_send()
                else:
                    copy.wait_recv()

        if toward:
            pl.when((sends if sent else gets)[toward])(wait)
        else:
            wait()

    pieces = 4
    chunk = slots // pieces
    jac_copies = [
        pltpu.make_async_copy(
            jac_in.at[q * chunk:(q + 1) * chunk], jac.at[q * chunk:(q + 1) * chunk], local_sem.at[q]
        )
        for q in range(pieces)
    ]
    kap_copy = pltpu.make_async_copy(
        kh_in, kap.at[MOST:MOST + cells_i, SIDE:SIDE + cells_j, :], local_sem.at[pieces]
    )
    small_copies = [
        pltpu.make_async_copy(src, dst, local_sem.at[pieces + 1 + q])
        for q, (src, dst) in enumerate(
            ((rows_hbm, rows_in), (innov_hbm, innov), (weight_hbm, weight), (kv_hbm, kv))
        )
    ]
    for copy in small_copies:
        copy.start()
    kap_copy.start()
    for copy in jac_copies:
        copy.start()

    partners = [(lat_of(i), lon_of(j)) for i, j in MOVES if i and j]
    partners += [(lat_of(d), b) for d in range(1, n_lat)]
    partners += [(a, lon_of(d)) for d in range(1, n_lon)]
    barrier = pltpu.get_barrier_semaphore()
    for to_lat, to_lon in partners:
        pl.semaphore_signal(
            barrier, inc=1, device_id=(to_lat, to_lon), device_id_type=pl.DeviceIdType.MESH
        )

    @pl.when(a == 0)
    def _():
        kap[0:MOST] = jnp.zeros((MOST, span, levels), F32)
        for field in range(5):
            ext[field, 0:MOST] = jnp.zeros((MOST, span, levels), F32)

    @pl.when(a == n_lat - 1)
    def _():
        kap[MOST + cells_i:] = jnp.zeros((MOST, span, levels), F32)
        for field in range(5):
            ext[field, MOST + cells_i:] = jnp.zeros((MOST, span, levels), F32)

    def packed(value):
        square[0:obs, 0:obs] = value
        turned = jnp.transpose(square[...])[0:obs, 0:obs]
        return jnp.concatenate([turned[0:half], turned[half:obs]], axis=1)

    square[...] = jnp.zeros(square.shape, F32)
    for copy in small_copies:
        copy.wait()
    wown[...] = packed(weight[...])
    band[0, core, chip] = wown[...] * packed(innov[...])

    pl.semaphore_wait(barrier, len(partners))
    kap_copy.wait()
    order = sorted(range(1, chips), key=lambda d: -min(d, chips - d))

    def send_band(r):
        mine = band.at[r, core, chip]
        sent = {
            d: remote(mine, mine, ag_s.at[r, d], ag_r.at[r, d], a, chip_of(d) * 2 + core)
            for d in order
        }
        return sent, [remote(mine, mine, fw_s.at[r, 0], fw_r.at[r, 0], a, sibling)]

    def forward_band(r, sent, forwards):
        for d in reversed(order):
            sent[d].wait_recv()
            arrived = band.at[r, core, chip_of(-d)]
            forwards.append(remote(arrived, arrived, fw_s.at[r, d], fw_r.at[r, d], a, sibling))
        return forwards

    def wait_band(forwards):
        for copy in forwards:
            copy.wait_recv()

    gathering = send_band(0)
    halo(kap, 0)

    lst[...] = jnp.full(lst.shape, n_lon * obs, jnp.int32)
    lst[0:2, 0:slots] = rows_in[...]
    padded = lst.shape[1]
    row_line = lst[0:1, :]
    col_line = lst[1:2, :]

    def upright(line):
        return jnp.transpose(jnp.broadcast_to(line.astype(F32), (128, padded))).astype(jnp.int32)

    def hot(test):
        return jnp.where(test, 1.0, 0.0).astype(BF16)

    lane = lax.broadcasted_iota(jnp.int32, (padded, 128), 1)
    sub = lax.broadcasted_iota(jnp.int32, (128, padded), 0)
    row_column = upright(row_line)
    col_column = upright(col_line)
    for j in range(2):
        for q in range(n_lon * half // 128):
            place = slice(128 * q, 128 * q + 128)
            rsel[j, :, place] = hot(row_column == 256 * q + half * j + obs * (lane // half) + lane % half)
            rselt[j, place, :] = hot(row_line == 256 * q + half * j + obs * (sub // half) + sub % half)
    for q in range(columns // 128):
        place = slice(128 * q, 128 * q + 128)
        chot[place, :] = hot((col_line == sub + 128 * q) & (row_line < n_lon * obs))
        chott[:, place] = hot(col_column == lane + 128 * q)
    contrib[slots:padded, :] = jnp.zeros((padded - slots, levels), F32)
    observed[slots:padded, :] = jnp.zeros((padded - slots, 128), F32)

    STEPS = levels // 8
    blocks = columns // 128

    def upended(q, value):
        turn_in[128 * q:128 * q + 128, :] = jnp.transpose(value)
        return [turn_in[pl.ds(128 * q + j, 8, stride=STEPS), :] for j in range(STEPS)]

    def restored(q, parts):
        for j in range(STEPS):
            turn_out[pl.ds(128 * q + j, 8, stride=STEPS), :] = parts[j]
        return jnp.transpose(turn_out[128 * q:128 * q + 128, :])

    def keep_parts(ref, q, parts):
        for j in range(STEPS):
            ref[128 * q + 8 * j:128 * q + 8 * j + 8, :] = parts[j]

    def kept(ref, q):
        return [ref[128 * q + 8 * j:128 * q + 8 * j + 8, :] for j in range(STEPS)]

    sublane = lax.broadcasted_iota(jnp.int32, (8, 128), 0)
    rows_each = 128 // cells_j
    for q in range(blocks):
        roots = [
            jnp.sqrt(part)
            for part in upended(q, kv[rows_each * q:rows_each * (q + 1)].reshape(128, levels))
        ]
        nexts = roots[1:] + [jnp.where(sublane < 7, pltpu.roll(roots[0], 7, 0), 0.0)]
        keep_parts(vco, q, [root * following for root, following in zip(roots, nexts)])

    forwards = None
    for q, copy in enumerate(jac_copies):
        if q == pieces - 1:
            forwards = forward_band(0, *gathering)
        copy.wait()

        @pl.loop(q * chunk // 4, (q + 1) * chunk // 4)
        def _(g):
            block = jac[pl.ds(4 * g, 4)].reshape(4 * obs, levels)
            place = pl.ds(pl.multiple_of(4 * obs * g, 4 * obs), 4 * obs)
            turned = pl.ds(pl.multiple_of(levels * g, levels), levels)
            jparts[0, place, :], jparts[1, place, :] = split(block)
            jturn[0, turned, :], jturn[1, turned, :] = split(jnp.transpose(block))


    lateral_count = jnp.full((span, levels), counts[0], jnp.int32)
    vertical_count = jnp.full((8, 128), counts[1], jnp.int32)

    def vertical(q, parts):
        for p in range(MOST):
            faces = kept(vco, q)
            uppers = parts[1:] + [pltpu.roll(parts[0], 7, 0)]
            flows = [face * (upper - w) for face, upper, w in zip(faces, uppers, parts)]
            lowers = [pltpu.roll(flows[-1], 1, 0)] + flows[:-1]
            news = [w + (flow - lower) for w, flow, lower in zip(parts, flows, lowers)]
            parts = news if p < LEAST else [
                jnp.where(vertical_count > p, new, w) for new, w in zip(news, parts)
            ]
        return parts

    def lateral(field, target):
        def rows_of(p, first, count):
            source = ext.at[field] if p == 0 else tmp.at[p - 1]
            ws = [source[first + q] for q in range(-1, count + 1)]
            flows = [lco[0, first + q - 1] * (ws[q + 1] - ws[q]) for q in range(count + 1)]
            news = []
            for q in range(count):
                w = ws[q + 1]
                east = lco[1, first + q] * (pltpu.roll(w, span - 1, 0) - w)
                new = w + (flows[q + 1] - flows[q]) + (east - pltpu.roll(east, 1, 0))
                news.append(new if p < LEAST else jnp.where(lateral_count > p, new, w))
            for q, new in enumerate(news):
                i = first + q
                if p < MOST - 1:
                    tmp[p, i] = new
                else:
                    place = (i - MOST) * cells_j
                    if not isinstance(place, int):
                        place = pl.multiple_of(place, cells_j)
                    target[pl.ds(place, cells_j), :] = new[SIDE:SIDE + cells_j, :]

        halo_wait(ext.at[field], field + 1, 0)
        for p in range(MOST):
            first = MOST + p + 1
            count = cells_i // 2 - p - 1

            @pl.loop(0, 2)
            def _(g, p=p, first=first, count=count):
                rows_of(p, first + count * g, count)

        halo_wait(ext.at[field], field + 1, -1)
        halo_wait(ext.at[field], field + 1, 1)
        for p in range(MOST):
            top = p + 1
            low = MOST + cells_i - p - 1

            @pl.loop(0, 2)
            def _(g, p=p, top=top, low=low):
                rows_of(p, top + (low - top) * g, MOST)


    def send_sum(i, tile, along_lat):
        sum_out[i] = tile
        count = n_lat if along_lat else n_lon
        return [
            remote(
                sum_out.at[i], sum_in.at[i, d - 1], sum_s.at[i, d - 1], sum_r.at[i, d - 1],
                lat_of(d) if along_lat else a, b if along_lat else lon_of(d),
            )
            for d in range(1, count)
        ]

    def take_sum(i, copies):
        for copy in copies:
            copy.wait_recv()
        tile = sum_out[i]
        for d in range(len(copies)):
            tile = tile + sum_in[i, d]
        return tile

    side8 = lax.broadcasted_iota(jnp.int32, (padded, 128), 0)
    lane8 = lax.broadcasted_iota(jnp.int32, (padded, 128), 1)
    quarter = side8 % 4
    left_block = lane8 // obs == quarter
    right_block = lane8 // obs + 2 == quarter
    first_half = side8 % 8 < 4
    low_lanes = lane8 < obs

    def put_lhs(part, left, right):
        lhs[part, :, 0:128] = left[0:slots]
        lhs[part, :, 128:256] = right[0:slots]

    def natural(part, g):
        first = 8 * obs * g
        return jnp.concatenate(
            [jparts[part, first:first + 4 * obs, :], jparts[part, first + 4 * obs:first + 8 * obs, :]],
            axis=1,
        )

    def turned(part, g):
        return jturn[part, 2 * levels * g:2 * levels * (g + 1), :]

    def products(matrix, finish):
        for g in range(slots // 8):
            place = slice(8 * g, 8 * g + 8)
            left = jnp.concatenate([lhs[0, place, :], lhs[1, place, :]], axis=0).astype(BF16)
            out = sum(jnp.dot(left, matrix(part, g), preferred_element_type=F32) for part in range(2))
            finish(place, out[0:8] + out[8:16])

    def adjoint(r, field):
        values = jnp.concatenate(
            [band[r, k, c] for c in range(chips) for k in range(2)], axis=0
        )
        picked = [pick(rsel[j], values) for j in range(2)]
        for part in range(2):
            taken = jnp.where(low_lanes, picked[0][part], picked[1][part])
            taken = taken + pltpu.roll(taken, obs, 1)
            put_lhs(part, jnp.where(left_block, taken, 0.0), jnp.where(right_block, taken, 0.0))

        def finish(place, out):
            contrib[place, :] = jnp.where(first_half[0:8], out[:, 0:128], out[:, 128:256])

        products(natural, finish)
        high, low = pick(chot[...], contrib[...])
        cells = high + low
        for i in range(cells_i):
            ext[field, MOST + i, SIDE:SIDE + cells_j, :] = cells[cells_j * i:cells_j * i + cells_j, :]

    def observe(which, r):
        picked = pick(chott[...], evolved[which])
        for part in range(2):
            put_lhs(part, jnp.where(first_half, picked[part], 0.0), jnp.where(first_half, 0.0, picked[part]))

        def finish(place, out):
            value = jnp.where(left_block[0:8], out[:, 0:128], 0.0) + jnp.where(
                right_block[0:8], out[:, 128:256], 0.0
            )
            observed[place, :] = value + pltpu.roll(value, obs, 1)

        products(turned, finish)
        high, low = zip(*(pick(rselt[j], observed[...]) for j in range(2)))
        narrow = lax.broadcasted_iota(jnp.int32, high[0].shape, 1) < obs
        partial = jnp.where(narrow, high[0] + low[0], high[1] + low[1])
        for c in range(chips):
            for k in range(2):
                first = half * (2 * c + k)
                zbuf[r, k, c] = partial[first:first + half, :]
        remote(zbuf.at[r, 1 - core], zsib.at[r], sib_s.at[r], sib_r.at[r], a, sibling).wait_recv()
        for c in range(chips):
            zchip[r, c] = zbuf[r, core, c] + zsib[r, c]
        copies = [
            remote(
                zchip.at[r, chip_of(d)], zin.at[r, d - 1], rs_s.at[r, d - 1], rs_r.at[r, d - 1],
                a, chip_of(d) * 2 + core,
            )
            for d in order
        ]
        total = zchip[r, chip]
        for copy in copies:
            copy.wait_recv()
        for d in range(1, chips):
            total = total + zin[r, d - 1]
        return total

    def fold(value):
        return jnp.sum(value.reshape(value.shape[0] // 8, 8, levels), axis=0)

    def stacked(parts):
        rows = lax.broadcasted_iota(jnp.int32, (8, levels), 0)
        tile = jnp.zeros((8, levels), F32)
        for i, part in enumerate(parts):
            tile = jnp.where(rows == i, jnp.sum(part, axis=0, keepdims=True), tile)
        return tile

    def entry(tile, i):
        return jnp.sum(tile[i:i + 1, :], axis=1, keepdims=True)

    wait_band(forwards)
    adjoint(0, 0)
    halo(ext.at[0], 1)

    for toward in (-1, 0, 1):
        halo_wait(kap, 0, toward)

    @pl.loop(0, total_rows // 2)
    def _(g):
        for u in range(2):
            tmp[0, 2 * g + u] = jnp.sqrt(kap[2 * g + u])

    @pl.loop(0, total_rows // 2)
    def _(g):
        for u in range(2):
            i = 2 * g + u
            root = tmp[0, i]
            lco[0, i] = root * tmp[0, jnp.minimum(i + 1, total_rows - 1)]
            lco[1, i] = root * pltpu.roll(root, span - 1, 0)

    def block_of(ref, q):
        return ref[128 * q:128 * q + 128, :]

    def middle(field, q, value):
        rows = slice(MOST + rows_each * q, MOST + rows_each * (q + 1))
        ext[field, rows, SIDE:SIDE + cells_j, :] = value.reshape(rows_each, cells_j, levels)

    def spread_and_send(field, work):
        accs = None
        for q in range(blocks):
            parts = work(q)
            accs = parts if accs is None else [x + y for x, y in zip(accs, parts)]
            if q == blocks // 2 - 1:
                halo_send(ext.at[field], field + 1, -1)
        halo_send(ext.at[field], field + 1, 1)
        halo_send(ext.at[field], field + 1, 0)
        return accs

    lateral(0, done)

    def gradient_block(q):
        ws = vertical(q, upended(q, block_of(done, q)))
        keep_parts(grad, q, ws)
        middle(1, q, restored(q, vertical(q, ws)))
        return [sum(w * w for w in ws)]

    (total,) = spread_and_send(1, gradient_block)
    lateral(1, evolved.at[0])

    piece = observe(0, 0)
    zown[...] = piece
    weighted = wown[...] * piece
    band[1, core, chip] = weighted
    gathering = send_band(1)
    sums_lat = send_sum(0, stacked([total, fold(weighted * piece)]), True)
    wait_band(forward_band(1, *gathering))
    adjoint(1, 2)
    halo(ext.at[2], 3)
    sums_lon = send_sum(1, take_sum(0, sums_lat), False)
    lateral(2, done)
    tile = take_sum(1, sums_lon)
    norm, curve = entry(tile, 0), entry(tile, 1)
    alpha_first = norm / (norm + curve)
    alpha_wide = jnp.broadcast_to(alpha_first, (8, 128))

    def residual_block(q):
        ws = vertical(q, upended(q, block_of(done, q)))
        gs = kept(grad, q)
        news = [g - alpha_wide * (g + w) for g, w in zip(gs, ws)]
        keep_parts(resid, q, news)
        keep_parts(image, q, ws)
        middle(3, q, restored(q, vertical(q, news)))
        return [sum(new * new for new in news), sum(new * g for new, g in zip(news, gs))]

    squares, crosses = spread_and_send(3, residual_block)
    lateral(3, evolved.at[1])

    piece = observe(1, 1)
    weighted = wown[...] * piece
    band[2, core, chip] = weighted
    gathering = send_band(2)
    sums_lat = send_sum(
        2, stacked([squares, crosses, fold(weighted * piece), fold(weighted * zown[...])]), True
    )
    wait_band(forward_band(2, *gathering))
    adjoint(2, 4)
    halo(ext.at[4], 5)
    sums_lon = send_sum(3, take_sum(2, sums_lat), False)
    lateral(4, done)
    tile = take_sum(3, sums_lon)
    norm_next, cross = entry(tile, 0), entry(tile, 1)
    beta = norm_next / norm
    self_product = norm_next + 2.0 * beta * cross + beta * beta * norm
    curve_next = entry(tile, 2) + 2.0 * beta * entry(tile, 3) + beta * beta * curve
    alpha_second = norm_next / (self_product + curve_next)
    second_wide = jnp.broadcast_to(alpha_second, (8, 128))
    beta_wide = jnp.broadcast_to(beta, (8, 128))
    for q in range(blocks):
        ws = vertical(q, upended(q, block_of(done, q)))
        lasts = [
            r - second_wide * (r + w + beta_wide * (g + v))
            for r, g, v, w in zip(kept(resid, q), kept(grad, q), kept(image, q), ws)
        ]
        rows = slice(rows_each * q, rows_each * (q + 1))
        residual_out[rows] = restored(q, lasts).reshape(rows_each, cells_j, levels)
    for i in range(cells_i):
        first = evolved[0, i * cells_j:(i + 1) * cells_j, :]
        second = evolved[1, i * cells_j:(i + 1) * cells_j, :]
        scale = alpha_first + alpha_second * beta
        increment[i] = scale * first + alpha_second * second

    for copy in started:
        copy.wait_send()
    for which in range(6):
        ref = kap if which == 0 else ext.at[which - 1]
        for toward in (-1, 0, 1):
            halo_wait(ref, which, toward, sent=True)


def hand_over(first, second, first_out, second_out, sems):
    copies = [
        pltpu.make_async_copy(first, first_out, sems.at[0]),
        pltpu.make_async_copy(second, second_out, sems.at[1]),
    ]
    for copy in copies:
        copy.start()
    for copy in copies:
        copy.wait()


def local(n_lat, n_lon, innovation, obs_weight, jacobian, block_list, pass_counts, kappa_h, kappa_v):
    cells_i, cells_j, levels = kappa_h.shape
    slots, obs, _ = jacobian.shape
    shape = (n_lat, n_lon, cells_i, cells_j, levels, slots, obs)
    chips = n_lon // 2
    half = obs // 2
    span = cells_j + 2 * SIDE
    total_rows = cells_i + 2 * MOST
    padded = -(-slots // 128) * 128
    columns = cells_i * cells_j
    peers = max(n_lat, n_lon) - 1
    vmem = pltpu.VMEM
    dma = pltpu.SemaphoreType.DMA
    field = jax.ShapeDtypeStruct((cells_i, cells_j, levels), F32)
    in_vmem = pl.BlockSpec(memory_space=pltpu.VMEM)
    in_smem = pl.BlockSpec(memory_space=pltpu.SMEM)
    in_any = pl.BlockSpec(memory_space=pl.ANY)
    results = pl.pallas_call(
        functools.partial(kernel, shape),
        out_shape=(field, field),
        in_specs=[in_smem] + [in_any] * 6,
        out_specs=(in_vmem, in_vmem),
        scratch_shapes=[
            vmem(block_list.shape, jnp.int32),
            vmem(innovation.shape, F32),
            vmem(obs_weight.shape, F32),
            vmem((cells_i, cells_j, levels), F32),
            vmem((slots, obs, levels), F32),
            vmem((2, slots * obs, levels), BF16),
            vmem((2, slots // 4 * levels, 4 * obs), BF16),
            vmem((total_rows, span, levels), F32),
            vmem((5, total_rows, span, levels), F32),
            vmem((MOST - 1, total_rows, span, levels), F32),
            vmem((2, total_rows, span, levels), F32),
            vmem((columns, levels), F32),
            vmem((8, padded), jnp.int32),
            vmem((2, padded, half * n_lon), BF16),
            vmem((2, half * n_lon, padded), BF16),
            vmem((columns, padded), BF16),
            vmem((padded, columns), BF16),
            vmem((2, slots, 256), F32),
            vmem((padded, levels), F32),
            vmem((padded, 128), F32),
            vmem((columns, levels), F32),
            vmem((columns, levels), F32),
            vmem((columns, levels), F32),
            vmem((columns, levels), F32),
            vmem((columns, levels), F32),
            vmem((columns, levels), F32),
            vmem((2, columns, levels), F32),
            vmem((128, 128), F32),
            vmem((2, 2, chips, half, 128), F32),
            vmem((2, chips, half, 128), F32),
            vmem((2, chips, half, 128), F32),
            vmem((2, chips - 1, half, 128), F32),
            vmem((half, 128), F32),
            vmem((half, 128), F32),
            vmem((3, 2, chips, half, 128), F32),
            vmem((4, 8, 128), F32),
            vmem((4, peers, 8, 128), F32),
            dma((9,)),
            dma((6, 8)), dma((6, 8)),
            dma((2,)), dma((2,)),
            dma((2, chips - 1)), dma((2, chips - 1)),
            dma((3, chips)), dma((3, chips)),
            dma((3, chips)), dma((3, chips)),
            dma((4, peers)), dma((4, peers)),
        ],
        compiler_params=pltpu.CompilerParams(
            collective_id=0, has_side_effects=True, vmem_limit_bytes=60 * 1024 * 1024
        ),
    )(pass_counts, block_list, innovation, obs_weight, jacobian, kappa_h, kappa_v)
    return pl.pallas_call(
        hand_over,
        out_shape=(field, field),
        in_specs=[in_vmem, in_vmem],
        out_specs=(in_any, in_any),
        scratch_shapes=[dma((2,))],
    )(*results)


def solution(mesh):
    return jax.shard_map(
        functools.partial(local, mesh.shape["lat"], mesh.shape["lon"]),
        mesh=mesh,
        in_specs=(
            P(None, ("lat", "lon")),
            P(None, ("lat", "lon")),
            P(("lat", "lon"), None, None),
            P(None, ("lat", "lon")),
            P(),
            P("lat", "lon", None),
            P("lat", "lon", None),
        ),
        out_specs=(P("lat", "lon", None), P("lat", "lon", None)),
        check_vma=False,
    )
```

```python
import functools

import jax
import jax.numpy as jnp
from jax import lax
from jax.experimental import pallas as pl
from jax.experimental.pallas import tpu as pltpu
from jax.sharding import PartitionSpec as P

MOST = 6
LEAST = 3
SIDE = 8
F32 = jnp.float32
BF16 = jnp.bfloat16
MOVES = tuple((i, j) for i in (-1, 0, 1) for j in (-1, 0, 1) if (i, j) != (0, 0))


def split(value):
    high = value.astype(BF16)
    return high, (value - high.astype(F32)).astype(BF16)


def pick(table, value):
    both = jnp.concatenate(split(value), axis=1)
    out = jnp.dot(table, both, preferred_element_type=F32)
    width = value.shape[1]
    return out[:, :width], out[:, width:]


def kernel(
    shape, counts, rows_hbm, innov_hbm, weight_hbm, jac_in, kh_in, kv_hbm,
    increment, residual_out,
    rows_in, innov, weight, kv, jac, jparts, jturn, kap, ext, tmp, lco, vco, lst, rsel, rselt, chot, chott, lhs, contrib, observed,
    done, grad, resid, image, turn_in, turn_out, evolved, square,
    zbuf, zsib, zchip, zin, zown, wown, band, sum_out, sum_in,
    local_sem, halo_s, halo_r, sib_s, sib_r, rs_s, rs_r,
    ag_s, ag_r, fw_s, fw_r, sum_s, sum_r,
):
    n_lat, n_lon, cells_i, cells_j, levels, slots, obs = shape
    chips = n_lon // 2
    half = obs // 2
    span = cells_j + 2 * SIDE
    total_rows = cells_i + 2 * MOST
    columns = cells_i * cells_j
    a = lax.axis_index("lat")
    b = lax.axis_index("lon")
    chip = b // 2
    core = lax.rem(b, 2)
    sibling = chip * 2 + 1 - core
    lat_of = lambda d: lax.rem(a + d + n_lat, n_lat)
    lon_of = lambda d: lax.rem(b + d + n_lon, n_lon)
    chip_of = lambda d: lax.rem(chip + d + chips, chips)
    started = []

    def describe(src, dst, ss, rs, to_lat, to_lon):
        return pltpu.make_async_remote_copy(
            src_ref=src, dst_ref=dst, send_sem=ss, recv_sem=rs,
            device_id=(to_lat, to_lon), device_id_type=pl.DeviceIdType.MESH,
        )

    def remote(*args):
        copy = describe(*args)
        copy.start()
        started.append(copy)
        return copy

    rows_src = {-1: slice(MOST, 2 * MOST), 0: slice(MOST, MOST + cells_i), 1: slice(cells_i, cells_i + MOST)}
    rows_dst = {-1: slice(MOST + cells_i, total_rows), 0: slice(MOST, MOST + cells_i), 1: slice(0, MOST)}
    cols_src = {-1: slice(SIDE, 2 * SIDE), 0: slice(SIDE, SIDE + cells_j), 1: slice(cells_j, cells_j + SIDE)}
    cols_dst = {-1: slice(SIDE + cells_j, span), 0: slice(SIDE, SIDE + cells_j), 1: slice(0, SIDE)}
    sends = {-1: a > 0, 1: a < n_lat - 1}
    gets = {-1: a < n_lat - 1, 1: a > 0}

    def halo_copy(ref, which, m):
        i, j = MOVES[m]
        return describe(
            ref.at[rows_src[i], cols_src[j], :], ref.at[rows_dst[i], cols_dst[j], :],
            halo_s.at[which, m], halo_r.at[which, m], lat_of(i), lon_of(j),
        )

    def halo_send(ref, which, toward):
        picked = [m for m in range(len(MOVES)) if MOVES[m][0] == toward]
        picked.sort(key=lambda m: MOVES[m][1] == 0)

        def start():
            for m in picked:
                halo_copy(ref, which, m).start()

        if toward:
            pl.when(sends[toward])(start)
        else:
            start()

    def halo(ref, which):
        for toward in (-1, 1, 0):
            halo_send(ref, which, toward)

    def halo_wait(ref, which, toward, sent=False):
        picked = [m for m in range(len(MOVES)) if MOVES[m][0] == toward]

        def wait():
            for m in picked:
                copy = halo_copy(ref, which, m)
                if sent:
                    copy.wait_send()
                else:
                    copy.wait_recv()

        if toward:
            pl.when((sends if sent else gets)[toward])(wait)
        else:
            wait()

    pieces = 4
    chunk = slots // pieces
    jac_copies = [
        pltpu.make_async_copy(
            jac_in.at[q * chunk:(q + 1) * chunk], jac.at[q * chunk:(q + 1) * chunk], local_sem.at[q]
        )
        for q in range(pieces)
    ]
    kap_copy = pltpu.make_async_copy(
        kh_in, kap.at[MOST:MOST + cells_i, SIDE:SIDE + cells_j, :], local_sem.at[pieces]
    )
    small_copies = [
        pltpu.make_async_copy(src, dst, local_sem.at[pieces + 1 + q])
        for q, (src, dst) in enumerate(
            ((rows_hbm, rows_in), (innov_hbm, innov), (weight_hbm, weight), (kv_hbm, kv))
        )
    ]
    for copy in small_copies:
        copy.start()
    kap_copy.start()
    for copy in jac_copies:
        copy.start()

    partners = [(lat_of(i), lon_of(j)) for i, j in MOVES if i and j]
    partners += [(lat_of(d), b) for d in range(1, n_lat)]
    partners += [(a, lon_of(d)) for d in range(1, n_lon)]
    barrier = pltpu.get_barrier_semaphore()
    for to_lat, to_lon in partners:
        pl.semaphore_signal(
            barrier, inc=1, device_id=(to_lat, to_lon), device_id_type=pl.DeviceIdType.MESH
        )

    @pl.when(a == 0)
    def _():
        kap[0:MOST] = jnp.zeros((MOST, span, levels), F32)
        for field in range(5):
            ext[field, 0:MOST] = jnp.zeros((MOST, span, levels), F32)

    @pl.when(a == n_lat - 1)
    def _():
        kap[MOST + cells_i:] = jnp.zeros((MOST, span, levels), F32)
        for field in range(5):
            ext[field, MOST + cells_i:] = jnp.zeros((MOST, span, levels), F32)

    def packed(value):
        square[0:obs, 0:obs] = value
        turned = jnp.transpose(square[...])[0:obs, 0:obs]
        return jnp.concatenate([turned[0:half], turned[half:obs]], axis=1)

    square[...] = jnp.zeros(square.shape, F32)
    for copy in small_copies:
        copy.wait()
    wown[...] = packed(weight[...])
    band[0, core, chip] = wown[...] * packed(innov[...])

    pl.semaphore_wait(barrier, len(partners))
    kap_copy.wait()
    order = sorted(range(1, chips), key=lambda d: -min(d, chips - d))

    def send_band(r):
        mine = band.at[r, core, chip]
        sent = {
            d: remote(mine, mine, ag_s.at[r, d], ag_r.at[r, d], a, chip_of(d) * 2 + core)
            for d in order
        }
        return sent, [remote(mine, mine, fw_s.at[r, 0], fw_r.at[r, 0], a, sibling)]

    def forward_band(r, sent, forwards):
        for d in reversed(order):
            sent[d].wait_recv()
            arrived = band.at[r, core, chip_of(-d)]
            forwards.append(remote(arrived, arrived, fw_s.at[r, d], fw_r.at[r, d], a, sibling))
        return forwards

    def wait_band(forwards):
        for copy in forwards:
            copy.wait_recv()

    gathering = send_band(0)
    halo(kap, 0)

    lst[...] = jnp.full(lst.shape, n_lon * obs, jnp.int32)
    lst[0:2, 0:slots] = rows_in[...]
    padded = lst.shape[1]
    row_line = lst[0:1, :]
    col_line = lst[1:2, :]

    def upright(line):
        return jnp.transpose(jnp.broadcast_to(line.astype(F32), (128, padded))).astype(jnp.int32)

    def hot(test):
        return jnp.where(test, 1.0, 0.0).astype(BF16)

    lane = lax.broadcasted_iota(jnp.int32, (padded, 128), 1)
    sub = lax.broadcasted_iota(jnp.int32, (128, padded), 0)
    row_column = upright(row_line)
    col_column = upright(col_line)
    for j in range(2):
        for q in range(n_lon * half // 128):
            place = slice(128 * q, 128 * q + 128)
            rsel[j, :, place] = hot(row_column == 256 * q + half * j + obs * (lane // half) + lane % half)
            rselt[j, place, :] = hot(row_line == 256 * q + half * j + obs * (sub // half) + sub % half)
    for q in range(columns // 128):
        place = slice(128 * q, 128 * q + 128)
        chot[place, :] = hot((col_line == sub + 128 * q) & (row_line < n_lon * obs))
        chott[:, place] = hot(col_column == lane + 128 * q)
    contrib[slots:padded, :] = jnp.zeros((padded - slots, levels), F32)
    observed[slots:padded, :] = jnp.zeros((padded - slots, 128), F32)

    STEPS = levels // 8
    blocks = columns // 128

    def upended(q, value):
        turn_in[128 * q:128 * q + 128, :] = jnp.transpose(value)
        return [turn_in[pl.ds(128 * q + j, 8, stride=STEPS), :] for j in range(STEPS)]

    def restored(q, parts):
        for j in range(STEPS):
            turn_out[pl.ds(128 * q + j, 8, stride=STEPS), :] = parts[j]
        return jnp.transpose(turn_out[128 * q:128 * q + 128, :])

    def keep_parts(ref, q, parts):
        for j in range(STEPS):
            ref[128 * q + 8 * j:128 * q + 8 * j + 8, :] = parts[j]

    def kept(ref, q):
        return [ref[128 * q + 8 * j:128 * q + 8 * j + 8, :] for j in range(STEPS)]

    sublane = lax.broadcasted_iota(jnp.int32, (8, 128), 0)
    rows_each = 128 // cells_j
    for q in range(blocks):
        roots = [
            jnp.sqrt(part)
            for part in upended(q, kv[rows_each * q:rows_each * (q + 1)].reshape(128, levels))
        ]
        nexts = roots[1:] + [jnp.where(sublane < 7, pltpu.roll(roots[0], 7, 0), 0.0)]
        keep_parts(vco, q, [root * following for root, following in zip(roots, nexts)])

    forwards = None
    for q, copy in enumerate(jac_copies):
        if q == pieces - 1:
            forwards = forward_band(0, *gathering)
        copy.wait()

        @pl.loop(q * chunk // 4, (q + 1) * chunk // 4)
        def _(g):
            block = jac[pl.ds(4 * g, 4)].reshape(4 * obs, levels)
            place = pl.ds(pl.multiple_of(4 * obs * g, 4 * obs), 4 * obs)
            turned = pl.ds(pl.multiple_of(levels * g, levels), levels)
            jparts[0, place, :], jparts[1, place, :] = split(block)
            jturn[0, turned, :], jturn[1, turned, :] = split(jnp.transpose(block))


    lateral_count = jnp.full((span, levels), counts[0], jnp.int32)
    vertical_count = jnp.full((8, 128), counts[1], jnp.int32)

    def vertical(q, parts):
        for p in range(MOST):
            faces = kept(vco, q)
            uppers = parts[1:] + [pltpu.roll(parts[0], 7, 0)]
            flows = [face * (upper - w) for face, upper, w in zip(faces, uppers, parts)]
            lowers = [pltpu.roll(flows[-1], 1, 0)] + flows[:-1]
            news = [w + (flow - lower) for w, flow, lower in zip(parts, flows, lowers)]
            parts = news if p < LEAST else [
                jnp.where(vertical_count > p, new, w) for new, w in zip(news, parts)
            ]
        return parts

    def lateral(field, target):
        def rows_of(p, first, count):
            source = ext.at[field] if p == 0 else tmp.at[p - 1]
            ws = [source[first + q] for q in range(-1, count + 1)]
            flows = [lco[0, first + q - 1] * (ws[q + 1] - ws[q]) for q in range(count + 1)]
            news = []
            for q in range(count):
                w = ws[q + 1]
                east = lco[1, first + q] * (pltpu.roll(w, span - 1, 0) - w)
                new = w + (flows[q + 1] - flows[q]) + (east - pltpu.roll(east, 1, 0))
                news.append(new if p < LEAST else jnp.where(lateral_count > p, new, w))
            for q, new in enumerate(news):
                i = first + q
                if p < MOST - 1:
                    tmp[p, i] = new
                else:
                    place = (i - MOST) * cells_j
                    if not isinstance(place, int):
                        place = pl.multiple_of(place, cells_j)
                    target[pl.ds(place, cells_j), :] = new[SIDE:SIDE + cells_j, :]

        halo_wait(ext.at[field], field + 1, 0)
        for p in range(MOST):
            first = MOST + p + 1
            count = cells_i // 2 - p - 1

            @pl.loop(0, 2)
            def _(g, p=p, first=first, count=count):
                rows_of(p, first + count * g, count)

        halo_wait(ext.at[field], field + 1, -1)
        halo_wait(ext.at[field], field + 1, 1)
        for p in range(MOST):
            top = p + 1
            low = MOST + cells_i - p - 1

            @pl.loop(0, 2)
            def _(g, p=p, top=top, low=low):
                rows_of(p, top + (low - top) * g, MOST)


    def send_sum(i, tile, along_lat):
        sum_out[i] = tile
        count = n_lat if along_lat else n_lon
        return [
            remote(
                sum_out.at[i], sum_in.at[i, d - 1], sum_s.at[i, d - 1], sum_r.at[i, d - 1],
                lat_of(d) if along_lat else a, b if along_lat else lon_of(d),
            )
            for d in range(1, count)
        ]

    def take_sum(i, copies):
        for copy in copies:
            copy.wait_recv()
        tile = sum_out[i]
        for d in range(len(copies)):
            tile = tile + sum_in[i, d]
        return tile

    side8 = lax.broadcasted_iota(jnp.int32, (padded, 128), 0)
    lane8 = lax.broadcasted_iota(jnp.int32, (padded, 128), 1)
    quarter = side8 % 4
    left_block = lane8 // obs == quarter
    right_block = lane8 // obs + 2 == quarter
    first_half = side8 % 8 < 4
    low_lanes = lane8 < obs

    def put_lhs(part, left, right):
        lhs[part, :, 0:128] = left[0:slots]
        lhs[part, :, 128:256] = right[0:slots]

    def natural(part, g):
        first = 8 * obs * g
        return jnp.concatenate(
            [jparts[part, first:first + 4 * obs, :], jparts[part, first + 4 * obs:first + 8 * obs, :]],
            axis=1,
        )

    def turned(part, g):
        return jturn[part, 2 * levels * g:2 * levels * (g + 1), :]

    def products(matrix, finish):
        for g in range(slots // 8):
            place = slice(8 * g, 8 * g + 8)
            left = jnp.concatenate([lhs[0, place, :], lhs[1, place, :]], axis=0).astype(BF16)
            out = sum(jnp.dot(left, matrix(part, g), preferred_element_type=F32) for part in range(2))
            finish(place, out[0:8] + out[8:16])

    def adjoint(r, field):
        values = jnp.concatenate(
            [band[r, k, c] for c in range(chips) for k in range(2)], axis=0
        )
        picked = [pick(rsel[j], values) for j in range(2)]
        for part in range(2):
            taken = jnp.where(low_lanes, picked[0][part], picked[1][part])
            taken = taken + pltpu.roll(taken, obs, 1)
            put_lhs(part, jnp.where(left_block, taken, 0.0), jnp.where(right_block, taken, 0.0))

        def finish(place, out):
            contrib[place, :] = jnp.where(first_half[0:8], out[:, 0:128], out[:, 128:256])

        products(natural, finish)
        high, low = pick(chot[...], contrib[...])
        cells = high + low
        for i in range(cells_i):
            ext[field, MOST + i, SIDE:SIDE + cells_j, :] = cells[cells_j * i:cells_j * i + cells_j, :]

    def observe(which, r):
        picked = pick(chott[...], evolved[which])
        for part in range(2):
            put_lhs(part, jnp.where(first_half, picked[part], 0.0), jnp.where(first_half, 0.0, picked[part]))

        def finish(place, out):
            value = jnp.where(left_block[0:8], out[:, 0:128], 0.0) + jnp.where(
                right_block[0:8], out[:, 128:256], 0.0
            )
            observed[place, :] = value + pltpu.roll(value, obs, 1)

        products(turned, finish)
        high, low = zip(*(pick(rselt[j], observed[...]) for j in range(2)))
        narrow = lax.broadcasted_iota(jnp.int32, high[0].shape, 1) < obs
        partial = jnp.where(narrow, high[0] + low[0], high[1] + low[1])
        for c in range(chips):
            for k in range(2):
                first = half * (2 * c + k)
                zbuf[r, k, c] = partial[first:first + half, :]
        halves = {}
        for d in order + [0]:
            c = chip_of(d)
            halves[d] = remote(
                zbuf.at[r, 1 - core, c], zsib.at[r, c], sib_s.at[r, d], sib_r.at[r, d], a, sibling
            )
        copies = []
        for d in order + [0]:
            c = chip_of(d)
            halves[d].wait_recv()
            zchip[r, c] = zbuf[r, core, c] + zsib[r, c]
            if d:
                copies.append(remote(
                    zchip.at[r, c], zin.at[r, d - 1], rs_s.at[r, d - 1], rs_r.at[r, d - 1],
                    a, c * 2 + core,
                ))
        total = zchip[r, chip]
        for copy in copies:
            copy.wait_recv()
        for d in range(1, chips):
            total = total + zin[r, d - 1]
        return total

    def fold(value):
        return jnp.sum(value.reshape(value.shape[0] // 8, 8, levels), axis=0)

    def stacked(parts):
        rows = lax.broadcasted_iota(jnp.int32, (8, levels), 0)
        tile = jnp.zeros((8, levels), F32)
        for i, part in enumerate(parts):
            tile = jnp.where(rows == i, jnp.sum(part, axis=0, keepdims=True), tile)
        return tile

    def entry(tile, i):
        return jnp.sum(tile[i:i + 1, :], axis=1, keepdims=True)

    wait_band(forwards)
    adjoint(0, 0)
    halo(ext.at[0], 1)

    for toward in (-1, 0, 1):
        halo_wait(kap, 0, toward)

    @pl.loop(0, total_rows // 2)
    def _(g):
        for u in range(2):
            tmp[0, 2 * g + u] = jnp.sqrt(kap[2 * g + u])

    @pl.loop(0, total_rows // 2)
    def _(g):
        for u in range(2):
            i = 2 * g + u
            root = tmp[0, i]
            lco[0, i] = root * tmp[0, jnp.minimum(i + 1, total_rows - 1)]
            lco[1, i] = root * pltpu.roll(root, span - 1, 0)

    def block_of(ref, q):
        return ref[128 * q:128 * q + 128, :]

    def middle(field, q, value):
        rows = slice(MOST + rows_each * q, MOST + rows_each * (q + 1))
        ext[field, rows, SIDE:SIDE + cells_j, :] = value.reshape(rows_each, cells_j, levels)

    def spread_and_send(field, work):
        accs = None
        for q in range(blocks):
            parts = work(q)
            accs = parts if accs is None else [x + y for x, y in zip(accs, parts)]
            if q == blocks // 2 - 1:
                halo_send(ext.at[field], field + 1, -1)
        halo_send(ext.at[field], field + 1, 1)
        halo_send(ext.at[field], field + 1, 0)
        return accs

    lateral(0, done)

    def gradient_block(q):
        ws = vertical(q, upended(q, block_of(done, q)))
        keep_parts(grad, q, ws)
        middle(1, q, restored(q, vertical(q, ws)))
        return [sum(w * w for w in ws)]

    (total,) = spread_and_send(1, gradient_block)
    lateral(1, evolved.at[0])

    piece = observe(0, 0)
    zown[...] = piece
    weighted = wown[...] * piece
    band[1, core, chip] = weighted
    gathering = send_band(1)
    sums_lat = send_sum(0, stacked([total, fold(weighted * piece)]), True)
    wait_band(forward_band(1, *gathering))
    adjoint(1, 2)
    halo(ext.at[2], 3)
    sums_lon = send_sum(1, take_sum(0, sums_lat), False)
    lateral(2, done)
    tile = take_sum(1, sums_lon)
    norm, curve = entry(tile, 0), entry(tile, 1)
    alpha_first = norm / (norm + curve)
    alpha_wide = jnp.broadcast_to(alpha_first, (8, 128))

    def residual_block(q):
        ws = vertical(q, upended(q, block_of(done, q)))
        gs = kept(grad, q)
        news = [g - alpha_wide * (g + w) for g, w in zip(gs, ws)]
        keep_parts(resid, q, news)
        keep_parts(image, q, ws)
        middle(3, q, restored(q, vertical(q, news)))
        return [sum(new * new for new in news), sum(new * g for new, g in zip(news, gs))]

    squares, crosses = spread_and_send(3, residual_block)
    lateral(3, evolved.at[1])

    piece = observe(1, 1)
    weighted = wown[...] * piece
    band[2, core, chip] = weighted
    gathering = send_band(2)
    sums_lat = send_sum(
        2, stacked([squares, crosses, fold(weighted * piece), fold(weighted * zown[...])]), True
    )
    wait_band(forward_band(2, *gathering))
    adjoint(2, 4)
    halo(ext.at[4], 5)
    sums_lon = send_sum(3, take_sum(2, sums_lat), False)
    lateral(4, done)
    tile = take_sum(3, sums_lon)
    norm_next, cross = entry(tile, 0), entry(tile, 1)
    beta = norm_next / norm
    self_product = norm_next + 2.0 * beta * cross + beta * beta * norm
    curve_next = entry(tile, 2) + 2.0 * beta * entry(tile, 3) + beta * beta * curve
    alpha_second = norm_next / (self_product + curve_next)
    second_wide = jnp.broadcast_to(alpha_second, (8, 128))
    beta_wide = jnp.broadcast_to(beta, (8, 128))
    for q in range(blocks):
        ws = vertical(q, upended(q, block_of(done, q)))
        lasts = [
            r - second_wide * (r + w + beta_wide * (g + v))
            for r, g, v, w in zip(kept(resid, q), kept(grad, q), kept(image, q), ws)
        ]
        rows = slice(rows_each * q, rows_each * (q + 1))
        residual_out[rows] = restored(q, lasts).reshape(rows_each, cells_j, levels)
    for i in range(cells_i):
        first = evolved[0, i * cells_j:(i + 1) * cells_j, :]
        second = evolved[1, i * cells_j:(i + 1) * cells_j, :]
        scale = alpha_first + alpha_second * beta
        increment[i] = scale * first + alpha_second * second

    for copy in started:
        copy.wait_send()
    for which in range(6):
        ref = kap if which == 0 else ext.at[which - 1]
        for toward in (-1, 0, 1):
            halo_wait(ref, which, toward, sent=True)


def hand_over(first, second, first_out, second_out, sems):
    copies = [
        pltpu.make_async_copy(first, first_out, sems.at[0]),
        pltpu.make_async_copy(second, second_out, sems.at[1]),
    ]
    for copy in copies:
        copy.start()
    for copy in copies:
        copy.wait()


def local(n_lat, n_lon, innovation, obs_weight, jacobian, block_list, pass_counts, kappa_h, kappa_v):
    cells_i, cells_j, levels = kappa_h.shape
    slots, obs, _ = jacobian.shape
    shape = (n_lat, n_lon, cells_i, cells_j, levels, slots, obs)
    chips = n_lon // 2
    half = obs // 2
    span = cells_j + 2 * SIDE
    total_rows = cells_i + 2 * MOST
    padded = -(-slots // 128) * 128
    columns = cells_i * cells_j
    peers = max(n_lat, n_lon) - 1
    vmem = pltpu.VMEM
    dma = pltpu.SemaphoreType.DMA
    field = jax.ShapeDtypeStruct((cells_i, cells_j, levels), F32)
    in_vmem = pl.BlockSpec(memory_space=pltpu.VMEM)
    in_smem = pl.BlockSpec(memory_space=pltpu.SMEM)
    in_any = pl.BlockSpec(memory_space=pl.ANY)
    results = pl.pallas_call(
        functools.partial(kernel, shape),
        out_shape=(field, field),
        in_specs=[in_smem] + [in_any] * 6,
        out_specs=(in_vmem, in_vmem),
        scratch_shapes=[
            vmem(block_list.shape, jnp.int32),
            vmem(innovation.shape, F32),
            vmem(obs_weight.shape, F32),
            vmem((cells_i, cells_j, levels), F32),
            vmem((slots, obs, levels), F32),
            vmem((2, slots * obs, levels), BF16),
            vmem((2, slots // 4 * levels, 4 * obs), BF16),
            vmem((total_rows, span, levels), F32),
            vmem((5, total_rows, span, levels), F32),
            vmem((MOST - 1, total_rows, span, levels), F32),
            vmem((2, total_rows, span, levels), F32),
            vmem((columns, levels), F32),
            vmem((8, padded), jnp.int32),
            vmem((2, padded, half * n_lon), BF16),
            vmem((2, half * n_lon, padded), BF16),
            vmem((columns, padded), BF16),
            vmem((padded, columns), BF16),
            vmem((2, slots, 256), F32),
            vmem((padded, levels), F32),
            vmem((padded, 128), F32),
            vmem((columns, levels), F32),
            vmem((columns, levels), F32),
            vmem((columns, levels), F32),
            vmem((columns, levels), F32),
            vmem((columns, levels), F32),
            vmem((columns, levels), F32),
            vmem((2, columns, levels), F32),
            vmem((128, 128), F32),
            vmem((2, 2, chips, half, 128), F32),
            vmem((2, chips, half, 128), F32),
            vmem((2, chips, half, 128), F32),
            vmem((2, chips - 1, half, 128), F32),
            vmem((half, 128), F32),
            vmem((half, 128), F32),
            vmem((3, 2, chips, half, 128), F32),
            vmem((4, 8, 128), F32),
            vmem((4, peers, 8, 128), F32),
            dma((9,)),
            dma((6, 8)), dma((6, 8)),
            dma((2, chips)), dma((2, chips)),
            dma((2, chips - 1)), dma((2, chips - 1)),
            dma((3, chips)), dma((3, chips)),
            dma((3, chips)), dma((3, chips)),
            dma((4, peers)), dma((4, peers)),
        ],
        compiler_params=pltpu.CompilerParams(
            collective_id=0, has_side_effects=True, vmem_limit_bytes=60 * 1024 * 1024
        ),
    )(pass_counts, block_list, innovation, obs_weight, jacobian, kappa_h, kappa_v)
    return pl.pallas_call(
        hand_over,
        out_shape=(field, field),
        in_specs=[in_vmem, in_vmem],
        out_specs=(in_any, in_any),
        scratch_shapes=[dma((2,))],
    )(*results)


def solution(mesh):
    return jax.shard_map(
        functools.partial(local, mesh.shape["lat"], mesh.shape["lon"]),
        mesh=mesh,
        in_specs=(
            P(None, ("lat", "lon")),
            P(None, ("lat", "lon")),
            P(("lat", "lon"), None, None),
            P(None, ("lat", "lon")),
            P(),
            P("lat", "lon", None),
            P("lat", "lon", None),
        ),
        out_specs=(P("lat", "lon", None), P("lat", "lon", None)),
        check_vma=False,
    )
```

```python
import functools

import jax
import jax.numpy as jnp
from jax import lax
from jax.experimental import pallas as pl
from jax.experimental.pallas import tpu as pltpu
from jax.sharding import PartitionSpec as P

MOST = 6
LEAST = 3
SIDE = 8
F32 = jnp.float32
BF16 = jnp.bfloat16
MOVES = tuple((i, j) for i in (-1, 0, 1) for j in (-1, 0, 1) if (i, j) != (0, 0))


def split(value):
    high = value.astype(BF16)
    return high, (value - high.astype(F32)).astype(BF16)


def pick(table, value):
    both = jnp.concatenate(split(value), axis=1)
    out = jnp.dot(table, both, preferred_element_type=F32)
    width = value.shape[1]
    return out[:, :width], out[:, width:]


def kernel(
    shape, counts, rows_hbm, innov_hbm, weight_hbm, jac_in, kh_in, kv_hbm,
    increment, residual_out,
    rows_in, innov, weight, kv, jac, jparts, jturn, kap, ext, tmp, lco, vco, lst, rsel, rselt, chot, chott, lhs, contrib, observed,
    done, grad, resid, image, turn_in, turn_out, evolved, square,
    zbuf, zsib, zchip, zin, zown, wown, band, sum_out, sum_in,
    local_sem, halo_s, halo_r, sib_s, sib_r, rs_s, rs_r,
    ag_s, ag_r, fw_s, fw_r, sum_s, sum_r,
):
    n_lat, n_lon, cells_i, cells_j, levels, slots, obs = shape
    chips = n_lon // 2
    half = obs // 2
    span = cells_j + 2 * SIDE
    total_rows = cells_i + 2 * MOST
    columns = cells_i * cells_j
    a = lax.axis_index("lat")
    b = lax.axis_index("lon")
    chip = b // 2
    core = lax.rem(b, 2)
    sibling = chip * 2 + 1 - core
    lat_of = lambda d: lax.rem(a + d + n_lat, n_lat)
    lon_of = lambda d: lax.rem(b + d + n_lon, n_lon)
    chip_of = lambda d: lax.rem(chip + d + chips, chips)
    started = []

    def describe(src, dst, ss, rs, to_lat, to_lon):
        return pltpu.make_async_remote_copy(
            src_ref=src, dst_ref=dst, send_sem=ss, recv_sem=rs,
            device_id=(to_lat, to_lon), device_id_type=pl.DeviceIdType.MESH,
        )

    def remote(*args):
        copy = describe(*args)
        copy.start()
        started.append(copy)
        return copy

    rows_src = {-1: slice(MOST, 2 * MOST), 0: slice(MOST, MOST + cells_i), 1: slice(cells_i, cells_i + MOST)}
    rows_dst = {-1: slice(MOST + cells_i, total_rows), 0: slice(MOST, MOST + cells_i), 1: slice(0, MOST)}
    cols_src = {-1: slice(SIDE, 2 * SIDE), 0: slice(SIDE, SIDE + cells_j), 1: slice(cells_j, cells_j + SIDE)}
    cols_dst = {-1: slice(SIDE + cells_j, span), 0: slice(SIDE, SIDE + cells_j), 1: slice(0, SIDE)}
    sends = {-1: a > 0, 1: a < n_lat - 1}
    gets = {-1: a < n_lat - 1, 1: a > 0}

    def halo_copy(ref, which, m):
        i, j = MOVES[m]
        return describe(
            ref.at[rows_src[i], cols_src[j], :], ref.at[rows_dst[i], cols_dst[j], :],
            halo_s.at[which, m], halo_r.at[which, m], lat_of(i), lon_of(j),
        )

    def halo_send(ref, which, toward):
        picked = [m for m in range(len(MOVES)) if MOVES[m][0] == toward]
        picked.sort(key=lambda m: MOVES[m][1] == 0)

        def start():
            for m in picked:
                halo_copy(ref, which, m).start()

        if toward:
            pl.when(sends[toward])(start)
        else:
            start()

    def halo(ref, which):
        for toward in (-1, 1, 0):
            halo_send(ref, which, toward)

    def halo_wait(ref, which, toward, sent=False):
        picked = [m for m in range(len(MOVES)) if MOVES[m][0] == toward]

        def wait():
            for m in picked:
                copy = halo_copy(ref, which, m)
                if sent:
                    copy.wait_send()
                else:
                    copy.wait_recv()

        if toward:
            pl.when((sends if sent else gets)[toward])(wait)
        else:
            wait()

    far_first = sorted(range(1, n_lon), key=lambda d: -min(d, n_lon - d))
    partners = [(a, lon_of(d)) for d in far_first]
    partners += [(lat_of(i), lon_of(j)) for i, j in MOVES if i and j]
    partners += [(lat_of(d), b) for d in range(1, n_lat)]
    barrier = pltpu.get_barrier_semaphore()
    for to_lat, to_lon in partners:
        pl.semaphore_signal(
            barrier, inc=1, device_id=(to_lat, to_lon), device_id_type=pl.DeviceIdType.MESH
        )

    pieces = 4
    chunk = slots // pieces
    jac_copies = [
        pltpu.make_async_copy(
            jac_in.at[q * chunk:(q + 1) * chunk], jac.at[q * chunk:(q + 1) * chunk], local_sem.at[q]
        )
        for q in range(pieces)
    ]
    kap_copy = pltpu.make_async_copy(
        kh_in, kap.at[MOST:MOST + cells_i, SIDE:SIDE + cells_j, :], local_sem.at[pieces]
    )
    small_copies = [
        pltpu.make_async_copy(src, dst, local_sem.at[pieces + 1 + q])
        for q, (src, dst) in enumerate(
            ((rows_hbm, rows_in), (innov_hbm, innov), (weight_hbm, weight), (kv_hbm, kv))
        )
    ]
    for copy in small_copies:
        copy.start()
    kap_copy.start()
    for copy in jac_copies:
        copy.start()

    @pl.when(a == 0)
    def _():
        kap[0:MOST] = jnp.zeros((MOST, span, levels), F32)
        for field in range(5):
            ext[field, 0:MOST] = jnp.zeros((MOST, span, levels), F32)

    @pl.when(a == n_lat - 1)
    def _():
        kap[MOST + cells_i:] = jnp.zeros((MOST, span, levels), F32)
        for field in range(5):
            ext[field, MOST + cells_i:] = jnp.zeros((MOST, span, levels), F32)

    def packed(value):
        square[0:obs, 0:obs] = value
        turned = jnp.transpose(square[...])[0:obs, 0:obs]
        return jnp.concatenate([turned[0:half], turned[half:obs]], axis=1)

    square[...] = jnp.zeros(square.shape, F32)
    for copy in small_copies:
        copy.wait()
    wown[...] = packed(weight[...])
    band[0, core, chip] = wown[...] * packed(innov[...])

    pl.semaphore_wait(barrier, len(partners))
    kap_copy.wait()
    order = sorted(range(1, chips), key=lambda d: -min(d, chips - d))

    def send_band(r):
        mine = band.at[r, core, chip]
        sent = {
            d: remote(mine, mine, ag_s.at[r, d], ag_r.at[r, d], a, chip_of(d) * 2 + core)
            for d in order
        }
        return sent, [remote(mine, mine, fw_s.at[r, 0], fw_r.at[r, 0], a, sibling)]

    def forward_band(r, sent, forwards):
        for d in reversed(order):
            sent[d].wait_recv()
            arrived = band.at[r, core, chip_of(-d)]
            forwards.append(remote(arrived, arrived, fw_s.at[r, d], fw_r.at[r, d], a, sibling))
        return forwards

    def wait_band(forwards):
        for copy in forwards:
            copy.wait_recv()

    gathering = send_band(0)
    halo(kap, 0)

    lst[...] = jnp.full(lst.shape, n_lon * obs, jnp.int32)
    lst[0:2, 0:slots] = rows_in[...]
    padded = lst.shape[1]
    row_line = lst[0:1, :]
    col_line = lst[1:2, :]

    def upright(line):
        return jnp.transpose(jnp.broadcast_to(line.astype(F32), (128, padded))).astype(jnp.int32)

    def hot(test):
        return jnp.where(test, 1.0, 0.0).astype(BF16)

    lane = lax.broadcasted_iota(jnp.int32, (padded, 128), 1)
    sub = lax.broadcasted_iota(jnp.int32, (128, padded), 0)
    row_column = upright(row_line)
    col_column = upright(col_line)
    for j in range(2):
        for q in range(n_lon * half // 128):
            place = slice(128 * q, 128 * q + 128)
            rsel[j, :, place] = hot(row_column == 256 * q + half * j + obs * (lane // half) + lane % half)
            rselt[j, place, :] = hot(row_line == 256 * q + half * j + obs * (sub // half) + sub % half)
    for q in range(columns // 128):
        place = slice(128 * q, 128 * q + 128)
        chot[place, :] = hot((col_line == sub + 128 * q) & (row_line < n_lon * obs))
        chott[:, place] = hot(col_column == lane + 128 * q)
    contrib[slots:padded, :] = jnp.zeros((padded - slots, levels), F32)
    observed[slots:padded, :] = jnp.zeros((padded - slots, 128), F32)

    STEPS = levels // 8
    blocks = columns // 128

    def upended(q, value):
        turn_in[128 * q:128 * q + 128, :] = jnp.transpose(value)
        return [turn_in[pl.ds(128 * q + j, 8, stride=STEPS), :] for j in range(STEPS)]

    def restored(q, parts):
        for j in range(STEPS):
            turn_out[pl.ds(128 * q + j, 8, stride=STEPS), :] = parts[j]
        return jnp.transpose(turn_out[128 * q:128 * q + 128, :])

    def keep_parts(ref, q, parts):
        for j in range(STEPS):
            ref[128 * q + 8 * j:128 * q + 8 * j + 8, :] = parts[j]

    def kept(ref, q):
        return [ref[128 * q + 8 * j:128 * q + 8 * j + 8, :] for j in range(STEPS)]

    sublane = lax.broadcasted_iota(jnp.int32, (8, 128), 0)
    rows_each = 128 // cells_j
    for q in range(blocks):
        roots = [
            jnp.sqrt(part)
            for part in upended(q, kv[rows_each * q:rows_each * (q + 1)].reshape(128, levels))
        ]
        nexts = roots[1:] + [jnp.where(sublane < 7, pltpu.roll(roots[0], 7, 0), 0.0)]
        keep_parts(vco, q, [root * following for root, following in zip(roots, nexts)])

    forwards = None
    for q, copy in enumerate(jac_copies):
        if q == pieces - 1:
            forwards = forward_band(0, *gathering)
        copy.wait()

        @pl.loop(q * chunk // 4, (q + 1) * chunk // 4)
        def _(g):
            block = jac[pl.ds(4 * g, 4)].reshape(4 * obs, levels)
            place = pl.ds(pl.multiple_of(4 * obs * g, 4 * obs), 4 * obs)
            turned = pl.ds(pl.multiple_of(levels * g, levels), levels)
            jparts[0, place, :], jparts[1, place, :] = split(block)
            jturn[0, turned, :], jturn[1, turned, :] = split(jnp.transpose(block))


    lateral_count = jnp.full((span, levels), counts[0], jnp.int32)
    vertical_count = jnp.full((8, 128), counts[1], jnp.int32)

    def vertical(q, parts):
        for p in range(MOST):
            faces = kept(vco, q)
            uppers = parts[1:] + [pltpu.roll(parts[0], 7, 0)]
            flows = [face * (upper - w) for face, upper, w in zip(faces, uppers, parts)]
            lowers = [pltpu.roll(flows[-1], 1, 0)] + flows[:-1]
            news = [w + (flow - lower) for w, flow, lower in zip(parts, flows, lowers)]
            parts = news if p < LEAST else [
                jnp.where(vertical_count > p, new, w) for new, w in zip(news, parts)
            ]
        return parts

    def lateral(field, target):
        def rows_of(p, first, count):
            source = ext.at[field] if p == 0 else tmp.at[p - 1]
            ws = [source[first + q] for q in range(-1, count + 1)]
            flows = [lco[0, first + q - 1] * (ws[q + 1] - ws[q]) for q in range(count + 1)]
            news = []
            for q in range(count):
                w = ws[q + 1]
                east = lco[1, first + q] * (pltpu.roll(w, span - 1, 0) - w)
                new = w + (flows[q + 1] - flows[q]) + (east - pltpu.roll(east, 1, 0))
                news.append(new if p < LEAST else jnp.where(lateral_count > p, new, w))
            for q, new in enumerate(news):
                i = first + q
                if p < MOST - 1:
                    tmp[p, i] = new
                else:
                    place = (i - MOST) * cells_j
                    if not isinstance(place, int):
                        place = pl.multiple_of(place, cells_j)
                    target[pl.ds(place, cells_j), :] = new[SIDE:SIDE + cells_j, :]

        halo_wait(ext.at[field], field + 1, 0)
        for p in range(MOST):
            first = MOST + p + 1
            count = cells_i // 2 - p - 1

            @pl.loop(0, 2)
            def _(g, p=p, first=first, count=count):
                rows_of(p, first + count * g, count)

        halo_wait(ext.at[field], field + 1, -1)
        halo_wait(ext.at[field], field + 1, 1)
        for p in range(MOST):
            top = p + 1
            low = MOST + cells_i - p - 1

            @pl.loop(0, 2)
            def _(g, p=p, top=top, low=low):
                rows_of(p, top + (low - top) * g, MOST)


    def send_sum(i, tile, along_lat):
        sum_out[i] = tile
        count = n_lat if along_lat else n_lon
        return [
            remote(
                sum_out.at[i], sum_in.at[i, d - 1], sum_s.at[i, d - 1], sum_r.at[i, d - 1],
                lat_of(d) if along_lat else a, b if along_lat else lon_of(d),
            )
            for d in range(1, count)
        ]

    def take_sum(i, copies):
        for copy in copies:
            copy.wait_recv()
        tile = sum_out[i]
        for d in range(len(copies)):
            tile = tile + sum_in[i, d]
        return tile

    side8 = lax.broadcasted_iota(jnp.int32, (padded, 128), 0)
    lane8 = lax.broadcasted_iota(jnp.int32, (padded, 128), 1)
    quarter = side8 % 4
    left_block = lane8 // obs == quarter
    right_block = lane8 // obs + 2 == quarter
    first_half = side8 % 8 < 4
    low_lanes = lane8 < obs

    def put_lhs(part, left, right):
        lhs[part, :, 0:128] = left[0:slots]
        lhs[part, :, 128:256] = right[0:slots]

    def natural(part, g):
        first = 8 * obs * g
        return jnp.concatenate(
            [jparts[part, first:first + 4 * obs, :], jparts[part, first + 4 * obs:first + 8 * obs, :]],
            axis=1,
        )

    def turned(part, g):
        return jturn[part, 2 * levels * g:2 * levels * (g + 1), :]

    def products(matrix, finish):
        for g in range(slots // 8):
            place = slice(8 * g, 8 * g + 8)
            left = jnp.concatenate([lhs[0, place, :], lhs[1, place, :]], axis=0).astype(BF16)
            out = sum(jnp.dot(left, matrix(part, g), preferred_element_type=F32) for part in range(2))
            finish(place, out[0:8] + out[8:16])

    def adjoint(r, field):
        values = jnp.concatenate(
            [band[r, k, c] for c in range(chips) for k in range(2)], axis=0
        )
        picked = [pick(rsel[j], values) for j in range(2)]
        for part in range(2):
            taken = jnp.where(low_lanes, picked[0][part], picked[1][part])
            taken = taken + pltpu.roll(taken, obs, 1)
            put_lhs(part, jnp.where(left_block, taken, 0.0), jnp.where(right_block, taken, 0.0))

        def finish(place, out):
            contrib[place, :] = jnp.where(first_half[0:8], out[:, 0:128], out[:, 128:256])

        products(natural, finish)
        high, low = pick(chot[...], contrib[...])
        cells = high + low
        for i in range(cells_i):
            ext[field, MOST + i, SIDE:SIDE + cells_j, :] = cells[cells_j * i:cells_j * i + cells_j, :]

    def observe(which, r):
        picked = pick(chott[...], evolved[which])
        for part in range(2):
            put_lhs(part, jnp.where(first_half, picked[part], 0.0), jnp.where(first_half, 0.0, picked[part]))

        def finish(place, out):
            value = jnp.where(left_block[0:8], out[:, 0:128], 0.0) + jnp.where(
                right_block[0:8], out[:, 128:256], 0.0
            )
            observed[place, :] = value + pltpu.roll(value, obs, 1)

        products(turned, finish)
        high, low = zip(*(pick(rselt[j], observed[...]) for j in range(2)))
        narrow = lax.broadcasted_iota(jnp.int32, high[0].shape, 1) < obs
        partial = jnp.where(narrow, high[0] + low[0], high[1] + low[1])
        for c in range(chips):
            for k in range(2):
                first = half * (2 * c + k)
                zbuf[r, k, c] = partial[first:first + half, :]
        halves = {}
        for d in order + [0]:
            c = chip_of(d)
            halves[d] = remote(
                zbuf.at[r, 1 - core, c], zsib.at[r, c], sib_s.at[r, d], sib_r.at[r, d], a, sibling
            )
        copies = []
        for d in order + [0]:
            c = chip_of(d)
            halves[d].wait_recv()
            zchip[r, c] = zbuf[r, core, c] + zsib[r, c]
            if d:
                copies.append(remote(
                    zchip.at[r, c], zin.at[r, d - 1], rs_s.at[r, d - 1], rs_r.at[r, d - 1],
                    a, c * 2 + core,
                ))
        total = zchip[r, chip]
        for copy in copies:
            copy.wait_recv()
        for d in range(1, chips):
            total = total + zin[r, d - 1]
        return total

    def fold(value):
        return jnp.sum(value.reshape(value.shape[0] // 8, 8, levels), axis=0)

    def stacked(parts):
        rows = lax.broadcasted_iota(jnp.int32, (8, levels), 0)
        tile = jnp.zeros((8, levels), F32)
        for i, part in enumerate(parts):
            tile = jnp.where(rows == i, jnp.sum(part, axis=0, keepdims=True), tile)
        return tile

    def entry(tile, i):
        return jnp.sum(tile[i:i + 1, :], axis=1, keepdims=True)

    wait_band(forwards)
    adjoint(0, 0)
    halo(ext.at[0], 1)

    for toward in (-1, 0, 1):
        halo_wait(kap, 0, toward)

    @pl.loop(0, total_rows // 2)
    def _(g):
        for u in range(2):
            tmp[0, 2 * g + u] = jnp.sqrt(kap[2 * g + u])

    @pl.loop(0, total_rows // 2)
    def _(g):
        for u in range(2):
            i = 2 * g + u
            root = tmp[0, i]
            lco[0, i] = root * tmp[0, jnp.minimum(i + 1, total_rows - 1)]
            lco[1, i] = root * pltpu.roll(root, span - 1, 0)

    def block_of(ref, q):
        return ref[128 * q:128 * q + 128, :]

    def middle(field, q, value):
        rows = slice(MOST + rows_each * q, MOST + rows_each * (q + 1))
        ext[field, rows, SIDE:SIDE + cells_j, :] = value.reshape(rows_each, cells_j, levels)

    def spread_and_send(field, work):
        accs = None
        for q in range(blocks):
            parts = work(q)
            accs = parts if accs is None else [x + y for x, y in zip(accs, parts)]
            if q == blocks // 2 - 1:
                halo_send(ext.at[field], field + 1, -1)
        halo_send(ext.at[field], field + 1, 1)
        halo_send(ext.at[field], field + 1, 0)
        return accs

    lateral(0, done)

    def gradient_block(q):
        ws = vertical(q, upended(q, block_of(done, q)))
        keep_parts(grad, q, ws)
        middle(1, q, restored(q, vertical(q, ws)))
        return [sum(w * w for w in ws)]

    (total,) = spread_and_send(1, gradient_block)
    lateral(1, evolved.at[0])

    piece = observe(0, 0)
    zown[...] = piece
    weighted = wown[...] * piece
    band[1, core, chip] = weighted
    gathering = send_band(1)
    sums_lat = send_sum(0, stacked([total, fold(weighted * piece)]), True)
    wait_band(forward_band(1, *gathering))
    adjoint(1, 2)
    halo(ext.at[2], 3)
    sums_lon = send_sum(1, take_sum(0, sums_lat), False)
    lateral(2, done)
    tile = take_sum(1, sums_lon)
    norm, curve = entry(tile, 0), entry(tile, 1)
    alpha_first = norm / (norm + curve)
    alpha_wide = jnp.broadcast_to(alpha_first, (8, 128))

    def residual_block(q):
        ws = vertical(q, upended(q, block_of(done, q)))
        gs = kept(grad, q)
        news = [g - alpha_wide * (g + w) for g, w in zip(gs, ws)]
        keep_parts(resid, q, news)
        keep_parts(image, q, ws)
        middle(3, q, restored(q, vertical(q, news)))
        return [sum(new * new for new in news), sum(new * g for new, g in zip(news, gs))]

    squares, crosses = spread_and_send(3, residual_block)
    lateral(3, evolved.at[1])

    piece = observe(1, 1)
    weighted = wown[...] * piece
    band[2, core, chip] = weighted
    gathering = send_band(2)
    sums_lat = send_sum(
        2, stacked([squares, crosses, fold(weighted * piece), fold(weighted * zown[...])]), True
    )
    wait_band(forward_band(2, *gathering))
    adjoint(2, 4)
    halo(ext.at[4], 5)
    sums_lon = send_sum(3, take_sum(2, sums_lat), False)
    lateral(4, done)
    tile = take_sum(3, sums_lon)
    norm_next, cross = entry(tile, 0), entry(tile, 1)
    beta = norm_next / norm
    self_product = norm_next + 2.0 * beta * cross + beta * beta * norm
    curve_next = entry(tile, 2) + 2.0 * beta * entry(tile, 3) + beta * beta * curve
    alpha_second = norm_next / (self_product + curve_next)
    second_wide = jnp.broadcast_to(alpha_second, (8, 128))
    beta_wide = jnp.broadcast_to(beta, (8, 128))
    for q in range(blocks):
        ws = vertical(q, upended(q, block_of(done, q)))
        lasts = [
            r - second_wide * (r + w + beta_wide * (g + v))
            for r, g, v, w in zip(kept(resid, q), kept(grad, q), kept(image, q), ws)
        ]
        rows = slice(rows_each * q, rows_each * (q + 1))
        residual_out[rows] = restored(q, lasts).reshape(rows_each, cells_j, levels)
    for i in range(cells_i):
        first = evolved[0, i * cells_j:(i + 1) * cells_j, :]
        second = evolved[1, i * cells_j:(i + 1) * cells_j, :]
        scale = alpha_first + alpha_second * beta
        increment[i] = scale * first + alpha_second * second

    for copy in started:
        copy.wait_send()
    for which in range(6):
        ref = kap if which == 0 else ext.at[which - 1]
        for toward in (-1, 0, 1):
            halo_wait(ref, which, toward, sent=True)


def hand_over(first, second, first_out, second_out, sems):
    copies = [
        pltpu.make_async_copy(first, first_out, sems.at[0]),
        pltpu.make_async_copy(second, second_out, sems.at[1]),
    ]
    for copy in copies:
        copy.start()
    for copy in copies:
        copy.wait()


def local(n_lat, n_lon, innovation, obs_weight, jacobian, block_list, pass_counts, kappa_h, kappa_v):
    cells_i, cells_j, levels = kappa_h.shape
    slots, obs, _ = jacobian.shape
    shape = (n_lat, n_lon, cells_i, cells_j, levels, slots, obs)
    chips = n_lon // 2
    half = obs // 2
    span = cells_j + 2 * SIDE
    total_rows = cells_i + 2 * MOST
    padded = -(-slots // 128) * 128
    columns = cells_i * cells_j
    peers = max(n_lat, n_lon) - 1
    vmem = pltpu.VMEM
    dma = pltpu.SemaphoreType.DMA
    field = jax.ShapeDtypeStruct((cells_i, cells_j, levels), F32)
    in_vmem = pl.BlockSpec(memory_space=pltpu.VMEM)
    in_smem = pl.BlockSpec(memory_space=pltpu.SMEM)
    in_any = pl.BlockSpec(memory_space=pl.ANY)
    results = pl.pallas_call(
        functools.partial(kernel, shape),
        out_shape=(field, field),
        in_specs=[in_smem] + [in_any] * 6,
        out_specs=(in_vmem, in_vmem),
        scratch_shapes=[
            vmem(block_list.shape, jnp.int32),
            vmem(innovation.shape, F32),
            vmem(obs_weight.shape, F32),
            vmem((cells_i, cells_j, levels), F32),
            vmem((slots, obs, levels), F32),
            vmem((2, slots * obs, levels), BF16),
            vmem((2, slots // 4 * levels, 4 * obs), BF16),
            vmem((total_rows, span, levels), F32),
            vmem((5, total_rows, span, levels), F32),
            vmem((MOST - 1, total_rows, span, levels), F32),
            vmem((2, total_rows, span, levels), F32),
            vmem((columns, levels), F32),
            vmem((8, padded), jnp.int32),
            vmem((2, padded, half * n_lon), BF16),
            vmem((2, half * n_lon, padded), BF16),
            vmem((columns, padded), BF16),
            vmem((padded, columns), BF16),
            vmem((2, slots, 256), F32),
            vmem((padded, levels), F32),
            vmem((padded, 128), F32),
            vmem((columns, levels), F32),
            vmem((columns, levels), F32),
            vmem((columns, levels), F32),
            vmem((columns, levels), F32),
            vmem((columns, levels), F32),
            vmem((columns, levels), F32),
            vmem((2, columns, levels), F32),
            vmem((128, 128), F32),
            vmem((2, 2, chips, half, 128), F32),
            vmem((2, chips, half, 128), F32),
            vmem((2, chips, half, 128), F32),
            vmem((2, chips - 1, half, 128), F32),
            vmem((half, 128), F32),
            vmem((half, 128), F32),
            vmem((3, 2, chips, half, 128), F32),
            vmem((4, 8, 128), F32),
            vmem((4, peers, 8, 128), F32),
            dma((9,)),
            dma((6, 8)), dma((6, 8)),
            dma((2, chips)), dma((2, chips)),
            dma((2, chips - 1)), dma((2, chips - 1)),
            dma((3, chips)), dma((3, chips)),
            dma((3, chips)), dma((3, chips)),
            dma((4, peers)), dma((4, peers)),
        ],
        compiler_params=pltpu.CompilerParams(
            collective_id=0, has_side_effects=True, vmem_limit_bytes=60 * 1024 * 1024
        ),
    )(pass_counts, block_list, innovation, obs_weight, jacobian, kappa_h, kappa_v)
    return pl.pallas_call(
        hand_over,
        out_shape=(field, field),
        in_specs=[in_vmem, in_vmem],
        out_specs=(in_any, in_any),
        scratch_shapes=[dma((2,))],
    )(*results)


def solution(mesh):
    return jax.shard_map(
        functools.partial(local, mesh.shape["lat"], mesh.shape["lon"]),
        mesh=mesh,
        in_specs=(
            P(None, ("lat", "lon")),
            P(None, ("lat", "lon")),
            P(("lat", "lon"), None, None),
            P(None, ("lat", "lon")),
            P(),
            P("lat", "lon", None),
            P("lat", "lon", None),
        ),
        out_specs=(P("lat", "lon", None), P("lat", "lon", None)),
        check_vma=False,
    )
```
